32 devices in a mesh: seq: 8 (over y, x, core), head: 4 (over z).
Axes of the slice: x: 2, y: 2, z: 4, core: 2. Of those that a mesh axis runs over, the one named last changes fastest.
Arguments:
- prefix_k: bfloat16 [8, 4096, 1024], P('seq', None, 'head'), may hold values from -7 to 7
- prefix_v: bfloat16 [8, 4096, 1024], P('seq', None, 'head'), may hold values from -6 to 6
- queries: bfloat16 [4096, 4096], P('seq', 'head'), may hold values from -100 to 100
- suffix_k: bfloat16 [4096, 1024], P('seq', 'head'), may hold values from -6 to 6
- suffix_v: bfloat16 [4096, 1024], P('seq', 'head'), may hold values from -6 to 6
- residual: bfloat16 [4096, 8192], P('seq', 'head'), may hold values from -12 to 12
- out_weight: bfloat16 [8192, 4096], P('seq', 'head'), may hold values from -2 to 2
- norm_gain: float32 [8192], replicated, may hold values from 0.25 to 1.75
- value_weight: float32 [8192], replicated, may hold values from -0.0029296875 to 0.0029296875
- prompt_of: int32 [8], replicated, may hold values from 0 to 7
- suffix_len: int32 [8], replicated, may hold values from 128 to 512
- return_table: float32 [512], replicated, may hold values from -4 to 4
- return_index: int32 [4096], P('seq'), may hold values from 0 to 511
Outputs:
- cache_k: bfloat16 [8, 4096, 1024], P(None, 'seq', 'head')
- cache_v: bfloat16 [8, 4096, 1024], P(None, 'seq', 'head')
- hidden: bfloat16 [4096, 8192], P('seq', 'head')
- values: float32 [4096], P('seq')
- grad_out: float32 [8192, 4096], P('seq', 'head')
The draws below stay inside these ranges and needn't reach their ends.
All inputs are finite; a program needn't handle non-finite values.
Results may differ from the reference program's by a relative error of at most 0.014.
Values may be sent and summed in bfloat16 or wider, within the bound.
No kernel may reach another device: no remote copies, remote signals or barrier semaphores. Data moves between devices by JAX's collectives and lax.ppermute only.
A program may use at most 192 MiB of HBM per device.

```python
import jax
import jax.numpy as jnp
from jax import lax

D = 8192
KVH = 8
HD = 128
HQ = 32
PLEN = 4096
SLEN = 512
BINS = 512
PROMPTS = 8
SUFFIXES = 8
TOKENS = 4096
N_SEQ = 8
N_HEAD = 4


def feature_signs(key):
    picked = jax.random.bernoulli(jax.random.fold_in(key, 601), 0.5, (D,))
    return jnp.where(picked, 1.0, -1.0).astype(jnp.float32)


def draw_value_weight(key, part):
    signs = feature_signs(key)
    size_key = jax.random.fold_in(key, 607)
    magnitude = jnp.minimum(jnp.abs(jax.random.normal(size_key, (D,), jnp.float32)), 4.0)
    return (signs * magnitude * (6.0 / D)).astype(jnp.float32)


def draw_prefix_k(key, part):
    shape = (PROMPTS, PLEN, KVH * HD)
    noise_key = jax.random.fold_in(key, 211)
    base = jnp.clip(jax.random.normal(noise_key, shape, jnp.float32), -6.0, 6.0)
    return base.astype(jnp.bfloat16)


def draw_queries(key, part):
    shape = (TOKENS, HQ * HD)
    noise_key = jax.random.fold_in(key, 401)
    base = 2.0 * jnp.clip(jax.random.normal(noise_key, shape, jnp.float32), -6.0, 6.0)
    return base.astype(jnp.bfloat16)


def draw_residual(key, part):
    shape = (TOKENS, D)
    column = jnp.arange(D).astype(jnp.float32) / D
    noise_key = jax.random.fold_in(key, 503)
    signs = feature_signs(key)
    token_size = jax.random.uniform(jax.random.fold_in(key, 613), (TOKENS, 1), jnp.float32, 0.5, 1.5)
    token_flip = jnp.where(jax.random.bernoulli(jax.random.fold_in(key, 617), 0.5, (TOKENS, 1)), 1.0, -1.0)
    leaning = 0.6 * token_size * token_flip * signs[None, :]
    base = jnp.clip(jax.random.normal(noise_key, shape, jnp.float32), -6.0, 6.0) * (0.7 + 0.5 * column)[None, :]
    return (base + leaning).astype(jnp.bfloat16)


def set_ends(values, rng, low, largest):
    extent = values.shape
    spot = [jax.random.randint(jax.random.fold_in(rng, axis), (), 0, extent[axis]) for axis in range(len(extent))]
    values = values.at[tuple(spot)].set(low)
    longest = extent.index(max(extent))
    spot[longest] = (spot[longest] + 1) % extent[longest]
    return values.at[tuple(spot)].set(largest)


def block_scale(own_key, shape, split, smallest, top_value):
    factor_of = 1.0
    for axis_at, parts in split:
        draws = jax.random.uniform(jax.random.fold_in(jax.random.fold_in(own_key, 6), axis_at), (parts,), jnp.float32, smallest / len(split), top_value / len(split))
        factor_of = factor_of * jnp.repeat(jnp.exp(draws), shape[axis_at] // parts).reshape((-1,) + (1,) * (len(shape) - 1 - axis_at))
    return factor_of


def bell_draw(rng, extent, scale, most, shards=(), kind=jnp.bfloat16):
    factor_of = block_scale(rng, extent, shards, -0.22, 0.18) if shards else 1.0
    entries = jax.random.normal(rng, extent, jnp.float32) * scale * factor_of
    return jnp.minimum(jnp.maximum(entries, -most), most).astype(kind)


def setup_inputs(seed: int = 0) -> dict:
    splits = jax.random.split(jax.random.key(seed), 14)
    return {
        "prefix_k": draw_prefix_k(jax.random.fold_in(splits[13], 71), 0),
        "prefix_v": bell_draw(splits[1], (PROMPTS, PLEN, KVH * HD), 1.0, 6.0, ((0, 8), (2, 4))),
        "queries": draw_queries(jax.random.fold_in(splits[13], 71), 0),
        "suffix_k": bell_draw(splits[3], (TOKENS, KVH * HD), 1.0, 6.0, ((0, 8), (1, 4))),
        "suffix_v": bell_draw(splits[4], (TOKENS, KVH * HD), 1.0, 6.0, ((0, 8), (1, 4))),
        "residual": draw_residual(jax.random.fold_in(splits[13], 71), 0),
        "out_weight": bell_draw(splits[6], (D, HQ * HD), 0.125, 2.0, ((0, 8), (1, 4))),
        "norm_gain": jnp.clip(1.0 + 0.15 * jax.random.normal(splits[7], (D,), jnp.float32), 0.25, 1.75),
        "value_weight": draw_value_weight(jax.random.fold_in(splits[13], 71), 0),
        "prompt_of": set_ends(jax.random.randint(splits[9], (SUFFIXES,), 0, PROMPTS), jax.random.fold_in(splits[9], 1), 0, PROMPTS - 1).astype(jnp.int32),
        "suffix_len": set_ends(jax.random.randint(splits[10], (SUFFIXES,), SLEN // 4, SLEN + 1), jax.random.fold_in(splits[10], 1), SLEN // 4, SLEN).astype(jnp.int32),
        "return_table": jnp.clip(jax.random.uniform(splits[11], (BINS,), jnp.float32, -4.0, 4.0), -4.0, 4.0),
        "return_index": set_ends(jax.random.randint(splits[12], (TOKENS,), 0, BINS), jax.random.fold_in(splits[12], 1), 0, BINS - 1).astype(jnp.int32),
    }


EPSILON = 1e-05
MASKED = -1e+30

def suffix_attention(query_rows, prompt_keys, prompt_values, own_keys, own_values):
    group_size = HQ // KVH
    key_rows = jnp.concatenate([prompt_keys, own_keys], 0).astype(jnp.float32).reshape(PLEN + SLEN, KVH, HD)
    value_rows = jnp.concatenate([prompt_values, own_values], 0).astype(jnp.float32).reshape(PLEN + SLEN, KVH, HD)
    query_block = query_rows.astype(jnp.float32).reshape(SLEN, KVH, group_size, HD)
    scores = jnp.einsum('skgd,lkd->kgsl', query_block, key_rows) * HD ** (-0.5)
    key_pos = jnp.arange(PLEN + SLEN)[None, :]
    query_pos = jnp.arange(SLEN)[:, None]
    allowed = (key_pos < PLEN) | (key_pos - PLEN <= query_pos)
    scores = jnp.where(allowed, scores, MASKED)
    row_max = lax.optimization_barrier(jnp.max(scores, -1, keepdims=True))
    weights = jnp.exp(scores - row_max)
    totals = lax.optimization_barrier(jnp.sum(weights, -1, keepdims=True))
    rounded = lax.optimization_barrier(weights.astype(jnp.bfloat16)).astype(jnp.float32)
    mixed = jnp.einsum('kgsl,lkd->skgd', rounded, value_rows)
    mixed = mixed / jnp.transpose(totals, (2, 0, 1, 3))
    return mixed.reshape(SLEN, HQ * HD).astype(jnp.bfloat16)

def reference(prefix_k, prefix_v, queries, suffix_k, suffix_v, residual, out_weight, norm_gain, value_weight, prompt_of, suffix_len, return_table, return_index):
    slab = HQ * HD // N_HEAD
    gain_weight = norm_gain * value_weight

    def one_suffix(carry, suffix_index):
        row_start = suffix_index * SLEN
        prompt = prompt_of[suffix_index]
        prompt_keys = lax.dynamic_index_in_dim(prefix_k, prompt, 0, keepdims=False)
        prompt_values = lax.dynamic_index_in_dim(prefix_v, prompt, 0, keepdims=False)
        query_rows = lax.dynamic_slice_in_dim(queries, row_start, SLEN, 0)
        own_keys = lax.dynamic_slice_in_dim(suffix_k, row_start, SLEN, 0)
        own_values = lax.dynamic_slice_in_dim(suffix_v, row_start, SLEN, 0)
        attn = suffix_attention(query_rows, prompt_keys, prompt_values, own_keys, own_values)
        summed = jnp.zeros((SLEN, D), jnp.float32)
        for group in range(N_HEAD):
            partial_value = jnp.dot(attn[:, group * slab:(group + 1) * slab], out_weight[:, group * slab:(group + 1) * slab].T, preferred_element_type=jnp.float32)
            summed = summed + lax.optimization_barrier(partial_value.astype(jnp.bfloat16)).astype(jnp.float32)
        residual_rows = lax.dynamic_slice_in_dim(residual, row_start, SLEN, 0)
        hidden_rows = (residual_rows.astype(jnp.float32) + summed).astype(jnp.bfloat16)
        hidden_wide = hidden_rows.astype(jnp.float32)
        square_sum = lax.optimization_barrier(jnp.sum(hidden_wide * hidden_wide, 1))
        weighted_sum = lax.optimization_barrier(jnp.sum(hidden_wide * gain_weight[None, :], 1))
        inverse = lax.rsqrt(square_sum / D + EPSILON)
        value_rows = weighted_sum * inverse
        index_rows = lax.dynamic_slice_in_dim(return_index, row_start, SLEN, 0)
        target = jnp.take(return_table, index_rows)
        live = jnp.arange(SLEN) < suffix_len[suffix_index]
        error_term = jnp.where(live, value_rows - target, 0.0)
        hidden_grad = (error_term[:, None] * (inverse[:, None] * gain_weight[None, :] - (weighted_sum * inverse * inverse * inverse)[:, None] * hidden_wide / D)).astype(jnp.bfloat16)
        term = jnp.dot(hidden_grad.T, attn, preferred_element_type=jnp.float32)
        return (carry + term, (hidden_rows, value_rows))
    grad_out, (hidden_all, value_all) = lax.scan(one_suffix, jnp.zeros((D, HQ * HD), jnp.float32), jnp.arange(N_SEQ, dtype=jnp.int32))
    return (prefix_k, prefix_v, hidden_all.reshape(TOKENS, D), value_all.reshape(TOKENS), grad_out)
```

```python
import functools
import math

import jax
import jax.numpy as jnp
from jax import lax
from jax.experimental import pallas as pl
from jax.experimental.pallas import tpu as pltpu
from jax.sharding import PartitionSpec as P


HD = 128
EPSILON = 1e-05
MASKED = -1e30
BF = jnp.bfloat16
F32 = jnp.float32
VMEM_LIMIT = 60 * 1024 * 1024


def tie(x, *deps):
    return lax.optimization_barrier((x, *deps))[0]


def shift_perm(count, step):
    return [(i, (i + step) % count) for i in range(count)]


def xor_perm(count, mask):
    return [(i, i ^ mask) for i in range(count)]


def dot_t(a, b):
    return lax.dot_general(a, b, (((1,), (1,)), ((), ())), preferred_element_type=F32)


def dot(a, b):
    return lax.dot_general(a, b, (((1,), (0,)), ((), ())), preferred_element_type=F32)


def attention_kernel(blocks, *refs):
    q_ref = refs[0]
    kv = refs[1 : 1 + blocks]
    sk_ref, sv_ref = refs[1 + blocks : 3 + blocks]
    o_ref, v_wide, scores = refs[-3:]
    tile = q_ref.shape[0]
    block_len = kv[0].shape[1]
    own_len = sk_ref.shape[0]
    prefix_len = blocks * block_len
    scale = HD ** (-0.5) / math.log(2.0)

    @pl.when((pl.program_id(0) == 0) & (pl.program_id(1) == 0))
    def _():
        for b in range(blocks):
            v_wide[b * block_len : (b + 1) * block_len, :HD] = kv[b][1]
        v_wide[prefix_len:, :HD] = sv_ref[...]
        v_wide[:, HD:] = jnp.ones((prefix_len + own_len, HD), BF)

    q = q_ref[...]
    spans = [(b * block_len, block_len) for b in range(blocks)]
    top = jnp.full((tile, HD), MASKED, F32)
    for b, (start, size) in enumerate(spans):
        s = dot_t(q, kv[b][0])
        scores[:, start : start + size] = s
        for lane in range(0, size, HD):
            top = jnp.maximum(top, s[:, lane : lane + HD])
    s = dot_t(q, sk_ref[...])
    row = lax.broadcasted_iota(jnp.int32, (tile, own_len), 0) + pl.program_id(1) * tile
    col = lax.broadcasted_iota(jnp.int32, (tile, own_len), 1)
    s = jnp.where(col <= row, s, MASKED)
    scores[:, prefix_len:] = s
    for lane in range(0, own_len, HD):
        top = jnp.maximum(top, s[:, lane : lane + HD])
    row_max = jnp.max(top, 1, keepdims=True)
    mixed = jnp.zeros((tile, 2 * HD), F32)
    for start, size in spans + [(prefix_len, own_len)]:
        p = jnp.exp2((scores[:, start : start + size] - row_max) * scale)
        mixed = mixed + dot(p.astype(BF), v_wide[start : start + size, :])
    o_ref[...] = (mixed[:, :HD] / mixed[:, HD:]).astype(BF)


def attention(queries, kv, suffix_k, suffix_v, head, group, first, count, before=None):
    rows = queries.shape[0]
    tile = 256
    blocks = len(kv)
    block_len = kv[0].shape[1]
    span = blocks * block_len + rows
    extra = [] if before is None else [before]
    return pl.pallas_call(
        functools.partial(attention_kernel, blocks),
        out_shape=jax.ShapeDtypeStruct((rows, group * HD), BF),
        grid=(count, rows // tile),
        in_specs=[pl.BlockSpec((tile, HD), lambda j, i: (i, head * group + first + j))]
        + [pl.BlockSpec(kv[0].shape, lambda j, i: (0, 0, 0))] * blocks
        + [pl.BlockSpec((rows, HD), lambda j, i: (0, head))] * 2
        + [pl.BlockSpec(memory_space=pl.ANY)] * len(extra),
        out_specs=pl.BlockSpec((tile, HD), lambda j, i: (i, first + j)),
        scratch_shapes=[pltpu.VMEM((span, 2 * HD), BF), pltpu.VMEM((tile, span), F32)],
        input_output_aliases={3 + blocks: 0} if extra else {},
        compiler_params=pltpu.CompilerParams(vmem_limit_bytes=VMEM_LIMIT),
        cost_estimate=pl.CostEstimate(
            flops=4 * rows * count * span * HD, bytes_accessed=4 * span * HD, transcendentals=rows * count * span
        ),
        name="attend",
    )(queries, *kv, suffix_k, suffix_v, *extra)


def route_kernel(count, head, *refs):
    pick, slot = refs[0], refs[1]
    came = refs[2 : 2 + count]
    outs = refs[-(count + 5) : -5]
    cache_k, cache_v, held, in_sem, out_sem = refs[-5:]
    for m in range(count):
        pltpu.make_async_copy(came[m], held.at[m], in_sem.at[m]).start()
    for m in range(count):
        pltpu.make_async_copy(came[m], held.at[m], in_sem.at[m]).wait()
    copies = [pltpu.make_async_copy(held.at[pick[m]], outs[m], out_sem.at[0, m]) for m in range(count)]
    cut = pl.ds(head * HD, HD)
    for which, cache in enumerate((cache_k, cache_v)):
        for m in range(count):
            copies.append(
                pltpu.make_async_copy(held.at[m, which], cache.at[slot[m], :, cut], out_sem.at[1 + which, m])
            )
    for copy in copies:
        copy.start()
    for copy in copies:
        copy.wait()


def route(pick, slot, came, head, kv_heads, caches):
    count = len(came)
    _, block_len, _ = came[0].shape
    cache = jax.ShapeDtypeStruct((count, block_len, kv_heads * HD), BF)
    smem_spec = pl.BlockSpec(memory_space=pltpu.SMEM)
    any_spec = pl.BlockSpec(memory_space=pl.ANY)
    extra = list(caches)
    outs = pl.pallas_call(
        functools.partial(route_kernel, count, head),
        out_shape=(jax.ShapeDtypeStruct(came[0].shape, BF),) * count + (cache, cache),
        in_specs=[smem_spec] * 2 + [any_spec] * (count + len(extra)),
        out_specs=(any_spec,) * (count + 2),
        scratch_shapes=[
            pltpu.VMEM((count, *came[0].shape), BF),
            pltpu.SemaphoreType.DMA((count,)),
            pltpu.SemaphoreType.DMA((3, count)),
        ],
        input_output_aliases={2 + count: count, 3 + count: count + 1} if extra else {},
        compiler_params=pltpu.CompilerParams(vmem_limit_bytes=VMEM_LIMIT),
        cost_estimate=pl.CostEstimate(flops=0, bytes_accessed=8 * 1024 * 1024, transcendentals=0),
        name="route",
    )(pick, slot, *came, *extra)
    return outs[:count], outs[count:]


def project_kernel(planes, parts, chips, *refs):
    pieces = planes * parts
    where_ref = refs[0]
    own = refs[1 : 1 + pieces]
    other = refs[1 + pieces : 1 + 2 * pieces]
    weights = refs[1 + 2 * pieces : 1 + 2 * pieces + 2 * chips]
    res_own, res_other, gain, h_own, h_other, h_flip, sums, a_buf, w_buf, a_sem, w_sem = refs[-11:]
    half = planes // 2
    width = own[0].shape[1]
    block = width * parts
    rows = own[0].shape[0]
    chip = where_ref[0]
    plane = where_ref[1]

    def a_copy(side, p):
        src = (own, other)[side][p]
        return pltpu.make_async_copy(src, a_buf.at[side, :, p * width : (p + 1) * width], a_sem.at[side, p])

    def w_copy(e, t):
        return pltpu.make_async_copy(
            weights[2 * e + t // half].at[t % half], w_buf.at[e, :, t * block : (t + 1) * block], w_sem.at[e, t]
        )

    for p in range(pieces):
        a_copy(0, p).start()
    for t in range(planes):
        w_copy(0, t).start()
    for p in range(pieces):
        a_copy(1, p).start()
    for e in range(1, chips):
        for t in range(planes):
            w_copy(e, t).start()
    for p in range(pieces):
        a_copy(0, p).wait()
    for p in range(pieces):
        a_copy(1, p).wait()
    sums[...] = jnp.zeros_like(sums)

    @pl.loop(0, chips)
    def _(e):
        for t in range(planes):
            landed = w_buf.at[e, :, t * block : (t + 1) * block]
            pltpu.make_async_copy(landed, landed, w_sem.at[e, t]).wait()
        home = jnp.bitwise_xor(chip, e)
        gain_col = gain[home]
        came = lax.rem(plane - home + planes, planes)
        goes = lax.rem(home - plane + planes, planes)
        for side, (res, out) in enumerate(((res_own, h_own), (res_other, h_other))):
            total = dot_t(a_buf[side], w_buf[e])
            h = (res[came].astype(F32) + total).astype(BF)
            out[goes] = h
            flip = h.astype(F32).T
            h_flip[e, :, side * rows : (side + 1) * rows] = flip.astype(BF)
            sums[2 * side : 2 * side + 1, :] += jnp.sum(flip * flip, 0, keepdims=True)
            sums[2 * side + 1 : 2 * side + 2, :] += jnp.sum(flip * gain_col, 0, keepdims=True)


def project(where, own, other, weights, res_own, res_other, gain, planes, parts):
    chips = len(weights) // 2
    rows, width = own[0].shape
    features = weights[0].shape[1]
    depth = planes * parts * width
    shape = jax.ShapeDtypeStruct
    any_spec = pl.BlockSpec(memory_space=pl.ANY)
    vmem_spec = pl.BlockSpec(memory_space=pltpu.VMEM)
    return pl.pallas_call(
        functools.partial(project_kernel, planes, parts, chips),
        out_shape=(
            shape((chips, rows, features), BF),
            shape((chips, rows, features), BF),
            shape((chips, features, 2 * rows), BF),
            shape((8, rows), F32),
        ),
        in_specs=[pl.BlockSpec(memory_space=pltpu.SMEM)]
        + [any_spec] * (2 * planes * parts + 2 * chips)
        + [vmem_spec] * 3,
        out_specs=(vmem_spec,) * 4,
        scratch_shapes=[
            pltpu.VMEM((2, rows, depth), BF),
            pltpu.VMEM((chips, features, depth), BF),
            pltpu.SemaphoreType.DMA((2, planes * parts)),
            pltpu.SemaphoreType.DMA((chips, planes)),
        ],
        compiler_params=pltpu.CompilerParams(vmem_limit_bytes=VMEM_LIMIT),
        cost_estimate=pl.CostEstimate(
            flops=4 * rows * features * chips * depth, bytes_accessed=24 * 1024 * 1024, transcendentals=0
        ),
        name="project",
    )(where, *own, *other, *weights, res_own, res_other, gain)


def gradient_kernel(parts, chips, *refs):
    grad = refs[0]
    own = refs[1 : 1 + parts]
    other = refs[1 + parts : 1 + 2 * parts]
    outs = refs[1 + 2 * parts :]
    rows, width = own[0].shape
    for e in range(chips):
        for g in range(parts):
            total = dot(grad[e, :, :rows], own[g][...]) + dot(grad[e, :, rows:], other[g][...])
            outs[e][:, g * width : (g + 1) * width] = total.astype(BF)


def gradient(grad, own, other):
    chips, features, tokens = grad.shape
    parts = len(own)
    width = own[0].shape[1]
    vmem_spec = pl.BlockSpec(memory_space=pltpu.VMEM)
    return pl.pallas_call(
        functools.partial(gradient_kernel, parts, chips),
        out_shape=(jax.ShapeDtypeStruct((features, parts * width), BF),) * chips,
        in_specs=[vmem_spec] * (1 + 2 * parts),
        out_specs=(vmem_spec,) * chips,
        compiler_params=pltpu.CompilerParams(vmem_limit_bytes=VMEM_LIMIT),
        cost_estimate=pl.CostEstimate(
            flops=2 * chips * features * tokens * parts * width, bytes_accessed=8 * 1024 * 1024, transcendentals=0
        ),
        name="gradient",
    )(grad, *own, *other)


def place_kernel(count, axis, size, *refs):
    where_ref = refs[0]
    out = refs[-1]
    for i in range(count):
        start = pl.multiple_of(where_ref[i] * size, size)
        piece = refs[1 + i][...].astype(out.dtype)
        if axis == 0:
            out[pl.ds(start, size), :] = piece
        else:
            out[:, pl.ds(start, size)] = piece


def place(slots, pieces, axis, dtype):
    shape = list(pieces[0].shape)
    size = shape[axis]
    if axis == 1 and size % HD:
        order = jnp.argsort(slots)
        stacked = jnp.take(jnp.stack(pieces, 0), order, axis=0, mode="clip")
        return jnp.concatenate([stacked[i] for i in range(len(pieces))], 1).astype(dtype)
    shape[axis] *= len(pieces)
    vmem_spec = pl.BlockSpec(memory_space=pltpu.VMEM)
    return pl.pallas_call(
        functools.partial(place_kernel, len(pieces), axis, size),
        out_shape=jax.ShapeDtypeStruct(tuple(shape), dtype),
        in_specs=[pl.BlockSpec(memory_space=pltpu.SMEM)] + [vmem_spec] * len(pieces),
        out_specs=vmem_spec,
        compiler_params=pltpu.CompilerParams(vmem_limit_bytes=VMEM_LIMIT),
        cost_estimate=pl.CostEstimate(flops=0, bytes_accessed=6 * 1024 * 1024, transcendentals=0),
        name="place",
    )(slots.astype(jnp.int32), *pieces)


def local(n_seq, n_head, prefix_k, prefix_v, queries, suffix_k, suffix_v, residual, out_weight,
          norm_gain, value_weight, prompt_of, suffix_len, return_table, return_index):
    chips = n_seq // 2
    bits = [1 << b for b in range(chips.bit_length() - 1)]
    rows = queries.shape[0]
    local_width = residual.shape[1]
    model = local_width * n_head
    kv_heads = prefix_k.shape[2] // HD
    group = queries.shape[1] // (kv_heads * HD)
    positions = prefix_k.shape[1]
    block_len = positions // n_seq
    seq = lax.axis_index("seq")
    plane = lax.axis_index("head")
    chip, core = seq // 2, seq % 2

    def seq_send(x, mask):
        return lax.ppermute(x, "seq", xor_perm(n_seq, mask))

    def partner(x):
        return seq_send(x, 1)

    def chip_send(x, bit):
        return seq_send(x, 2 * bit)

    def plane_send(x, step):
        return lax.ppermute(x, "head", shift_perm(n_head, step))

    def next_plane(step):
        return (plane + step) % n_head

    def plane_send(x, step):
        return lax.ppermute(x, "head", shift_perm(n_head, step))

    def next_plane(step):
        return (plane + step) % n_head

    peers = [seq ^ m for m in range(n_seq)]
    moved = []
    for head in range(kv_heads):
        cut = slice(head * HD, (head + 1) * HD)
        came = []
        for m, peer in enumerate(peers):
            k, v = (
                lax.dynamic_slice_in_dim(source[0, :, cut], peer * block_len, block_len, 0)
                for source in (prefix_k, prefix_v)
            )
            piece = jnp.stack([k, v], 0)
            came.append(seq_send(piece, m) if m else piece)
        moved.append(came)

    weight_rows = out_weight.shape[0] // n_head
    w_own = []
    for t in range(n_head):
        piece = lax.dynamic_slice_in_dim(out_weight, next_plane(t) * weight_rows, weight_rows, 0)
        w_own.append(plane_send(piece, t) if t else piece)
    w_own = [jnp.stack(w_own[: n_head // 2], 0), jnp.stack(w_own[n_head // 2 :], 0)]

    res = residual.reshape(rows, 2, n_head, weight_rows)
    res_own, res_other = [], []
    for t in range(n_head):
        piece = lax.dynamic_index_in_dim(res, next_plane(t), 2, keepdims=False)
        mine = lax.dynamic_index_in_dim(piece, core, 1, keepdims=False)
        yours = lax.dynamic_index_in_dim(piece, 1 - core, 1, keepdims=False)
        if t:
            both = tie(jnp.stack([mine, yours], 0), *w_own)
            both = plane_send(both, t)
            mine, yours = both[0], both[1]
        res_own.append(mine)
        res_other.append(yours)
    res_own = jnp.stack(res_own, 0)
    res_other = partner(jnp.stack(res_other, 0))

    gain_weight = norm_gain * value_weight
    gain = gain_weight.reshape(chips, 2, n_head, weight_rows)
    gain = lax.dynamic_index_in_dim(gain, core, 1, keepdims=False)
    gain = lax.dynamic_index_in_dim(gain, plane, 1, keepdims=False)

    bins = return_table.shape[0]
    one_hot = return_index[:, None] == jnp.arange(bins)[None, :]
    target = jnp.sum(jnp.where(one_hot, return_table[None, :], 0.0), 1)
    target_other = partner(target)

    slot = jnp.stack(peers).astype(jnp.int32)
    pick = (jnp.take(prompt_of, slot, mode="clip") ^ seq).astype(jnp.int32)
    attn = []
    caches = ()
    begun = None
    count = max(group // 2, 1)
    for head in range(kv_heads):
        came = moved[head]
        if begun is not None:
            came = list(lax.optimization_barrier((*came, begun))[:-1])
        chosen, caches = route(pick, slot, came, head, kv_heads, caches)
        kv = [chosen[0]] + [seq_send(c, m) for m, c in enumerate(chosen) if m]
        part = None
        for step, first in enumerate(range(0, group, count)):
            part = attention(queries, kv, suffix_k, suffix_v, head, group, first, count, part)
            if not step:
                begun = part
        attn.append(part)
    cache_k, cache_v = caches

    w_own = list(lax.optimization_barrier((*w_own, *kv))[:2])
    weights = [w_own] + [None] * (chips - 1)
    for e in sorted(range(1, chips), key=lambda v: bin(v).count("1")):
        low, high = e & -e, 1 << (e.bit_length() - 1)
        if low == high:
            pair = [None, None]
            for part in (1, 0) if low == 1 else (0, 1):
                pair[part] = chip_send(w_own[part], e)
            weights[e] = pair
        else:
            weights[e] = [chip_send(weights[e ^ low][0], low), chip_send(weights[e ^ high][1], high)]

    own = [[None] * kv_heads for _ in range(n_head)]
    other = [[None] * kv_heads for _ in range(n_head)]
    for g in range(kv_heads):
        piece = attn[g]
        for t in range(n_head):
            own[t][g] = piece
            other[t][g] = partner(piece)
            if t + 1 < n_head:
                piece = plane_send(piece, 1)

    where = jnp.stack([chip, plane]).astype(jnp.int32)
    h_own, h_other, h_flip, sums = project(
        where, sum(own, []), sum(other, []), sum(weights, []), res_own, res_other, gain[:, :, None], n_head, kv_heads
    )

    h_rest = partner(h_other)
    back, slots = [], []
    for side, source in ((core, h_own), (1 - core, h_rest)):
        for t in range(n_head):
            back.append(plane_send(source[t], t) if t else source[0])
            slots.append(side * n_head + next_plane(-t))
    hidden = place(jnp.stack(slots), back, 1, BF)

    mine, yours = sums[:4], partner(sums[:4])
    totals = mine + jnp.concatenate([yours[2:], yours[:2]], 0)
    step = 1
    while step < n_head:
        totals = totals + lax.ppermute(totals, "head", xor_perm(n_head, step))
        step *= 2
    square_sum = jnp.concatenate([totals[0], totals[2]])
    weighted_sum = jnp.concatenate([totals[1], totals[3]])
    inverse = lax.rsqrt(square_sum / model + EPSILON)
    value_rows = weighted_sum * inverse
    targets = jnp.concatenate([target, target_other])
    position = jnp.arange(rows)
    live = jnp.concatenate([position < suffix_len[seq], position < suffix_len[seq ^ 1]])
    error = jnp.where(live, value_rows - targets, 0.0)
    first_term = error * inverse
    second_term = error * (weighted_sum * inverse * inverse * inverse) / model
    gain_near = jnp.take(gain, chip ^ jnp.arange(chips), axis=0, mode="clip")
    grad = (
        first_term[None, None, :] * gain_near[:, :, None] - second_term[None, None, :] * h_flip.astype(F32)
    ).astype(BF)

    final = []
    for t in [*range(1, n_head), 0]:
        terms = list(gradient(grad, own[t], other[t]))
        order = bits if t % 2 else bits[::-1]
        alive = list(range(chips))
        for bit in order:
            got = {}
            for e in alive:
                if e & bit:
                    got[e ^ bit] = chip_send(terms[e], bit)
            alive = [e for e in alive if not e & bit]
            for e in alive:
                terms[e] = (terms[e].astype(F32) + got[e].astype(F32)).astype(BF)
        final.append(plane_send(terms[0], -t) if t else terms[0])
    final = final[-1:] + final[:-1]
    grad_out = place(jnp.stack([next_plane(t) for t in range(n_head)]), final, 0, F32)
    return (cache_k, cache_v, hidden, value_rows[:rows], grad_out)


def solution(mesh):
    in_specs = (
        P("seq", None, "head"),
        P("seq", None, "head"),
        P("seq", "head"),
        P("seq", "head"),
        P("seq", "head"),
        P("seq", "head"),
        P("seq", "head"),
        P(),
        P(),
        P(),
        P(),
        P(),
        P("seq"),
    )
    out_specs = (
        P(None, "seq", "head"),
        P(None, "seq", "head"),
        P("seq", "head"),
        P("seq"),
        P("seq", "head"),
    )
    body = functools.partial(local, mesh.shape["seq"], mesh.shape["head"])

    return jax.shard_map(body, mesh=mesh, in_specs=in_specs, out_specs=out_specs, check_vma=False)
```

```python
import functools
import math

import jax
import jax.numpy as jnp
from jax import lax
from jax.experimental import pallas as pl
from jax.experimental.pallas import tpu as pltpu
from jax.sharding import PartitionSpec as P


HD = 128
EPSILON = 1e-05
MASKED = -1e30
BF = jnp.bfloat16
F32 = jnp.float32
TILE = 256
VMEM_LIMIT = 60 * 1024 * 1024


def tie(x, *deps):
    return lax.optimization_barrier((x, *deps))[0]


def shift_perm(count, step):
    return [(i, (i + step) % count) for i in range(count)]


def xor_perm(count, mask):
    return [(i, i ^ mask) for i in range(count)]


def dot_t(a, b):
    return lax.dot_general(a, b, (((1,), (1,)), ((), ())), preferred_element_type=F32)


def dot(a, b):
    return lax.dot_general(a, b, (((1,), (0,)), ((), ())), preferred_element_type=F32)


def attention_kernel(q_ref, kv, sk_ref, sv_ref, o_ref, v_wide, scores):
    blocks = kv.shape[0]
    tile = q_ref.shape[0]
    block_len = kv.shape[2]
    own_len = sk_ref.shape[0]
    prefix_len = blocks * block_len
    scale = HD ** (-0.5) / math.log(2.0)

    @pl.when((pl.program_id(0) == 0) & (pl.program_id(1) == 0))
    def _():
        for b in range(blocks):
            v_wide[b * block_len : (b + 1) * block_len, :HD] = kv[b, 1]
        v_wide[prefix_len:, :HD] = sv_ref[...]
        v_wide[:, HD:] = jnp.ones((prefix_len + own_len, HD), BF)

    q = q_ref[...]
    spans = [(b * block_len, block_len) for b in range(blocks)]
    top = jnp.full((tile, HD), MASKED, F32)
    for b, (start, size) in enumerate(spans):
        s = dot_t(q, kv[b, 0])
        scores[:, start : start + size] = s
        for lane in range(0, size, HD):
            top = jnp.maximum(top, s[:, lane : lane + HD])
    s = dot_t(q, sk_ref[...])
    row = lax.broadcasted_iota(jnp.int32, (tile, own_len), 0) + pl.program_id(1) * tile
    col = lax.broadcasted_iota(jnp.int32, (tile, own_len), 1)
    s = jnp.where(col <= row, s, MASKED)
    scores[:, prefix_len:] = s
    for lane in range(0, own_len, HD):
        top = jnp.maximum(top, s[:, lane : lane + HD])
    row_max = jnp.max(top, 1, keepdims=True)
    mixed = jnp.zeros((tile, 2 * HD), F32)
    for start, size in spans + [(prefix_len, own_len)]:
        p = jnp.exp2((scores[:, start : start + size] - row_max) * scale)
        mixed = mixed + dot(p.astype(BF), v_wide[start : start + size, :])
    o_ref[...] = (mixed[:, :HD] / mixed[:, HD:]).astype(BF)


def attention(queries, kv, suffix_k, suffix_v, head, group, first, count):
    rows = queries.shape[0]
    tile = TILE
    blocks, _, block_len, _ = kv.shape
    span = blocks * block_len + rows
    return pl.pallas_call(
        attention_kernel,
        out_shape=jax.ShapeDtypeStruct((rows, count * HD), BF),
        grid=(count, rows // tile),
        in_specs=[pl.BlockSpec((tile, HD), lambda j, i: (i, head * group + first + j))]
        + [pl.BlockSpec(kv.shape, lambda j, i: (0, 0, 0, 0))]
        + [pl.BlockSpec((rows, HD), lambda j, i: (0, head))] * 2,
        out_specs=pl.BlockSpec((tile, HD), lambda j, i: (i, j)),
        scratch_shapes=[pltpu.VMEM((span, 2 * HD), BF), pltpu.VMEM((tile, span), F32)],
        compiler_params=pltpu.CompilerParams(vmem_limit_bytes=VMEM_LIMIT),
        cost_estimate=pl.CostEstimate(
            flops=4 * rows * count * span * HD, bytes_accessed=4 * span * HD, transcendentals=rows * count * span
        ),
        name="attend",
    )(queries, kv, suffix_k, suffix_v)


def route_kernel(head, *refs):
    pick, came = refs[:2]
    chosen, cache_k, cache_v, held, in_sem, out_sem, cache_sem = refs[-7:]
    count = held.shape[0]
    load = pltpu.make_async_copy(came, held, in_sem)
    load.start()
    load.wait()
    cut = pl.ds(head * HD, HD)
    copies = [pltpu.make_async_copy(held.at[pick[n]], chosen.at[n], out_sem.at[n]) for n in range(count)]
    for which, cache in enumerate((cache_k, cache_v)):
        copies.append(pltpu.make_async_copy(held.at[:, which], cache.at[:, :, cut], cache_sem.at[which]))
    for copy in copies:
        copy.start()
    for copy in copies:
        copy.wait()


def route(pick, came, head, kv_heads, caches):
    count, _, block_len, _ = came.shape
    cache = jax.ShapeDtypeStruct((count, block_len, kv_heads * HD), BF)
    any_spec = pl.BlockSpec(memory_space=pl.ANY)
    extra = list(caches)
    chosen, *caches = pl.pallas_call(
        functools.partial(route_kernel, head),
        out_shape=(jax.ShapeDtypeStruct(came.shape, BF), cache, cache),
        in_specs=[pl.BlockSpec(memory_space=pltpu.SMEM)] + [any_spec] * (1 + len(extra)),
        out_specs=(any_spec,) * 3,
        scratch_shapes=[
            pltpu.VMEM(came.shape, BF),
            pltpu.SemaphoreType.DMA,
            pltpu.SemaphoreType.DMA((count,)),
            pltpu.SemaphoreType.DMA((2,)),
        ],
        input_output_aliases={2: 1, 3: 2} if extra else {},
        compiler_params=pltpu.CompilerParams(vmem_limit_bytes=VMEM_LIMIT),
        cost_estimate=pl.CostEstimate(flops=0, bytes_accessed=8 * 1024 * 1024, transcendentals=0),
        name="route",
    )(pick, came, *extra)
    return chosen, caches


def fill(planes, widths, sides, weights, a_buf, w_buf, a_sem, w_sem, more):
    parts = len(widths)
    block = sum(widths)
    chips = len(weights) // planes
    copies = []
    for side in range(2):
        for t in range(planes):
            for g in range(parts):
                start = t * block + sum(widths[:g])
                copies.append(
                    pltpu.make_async_copy(
                        sides[side][t * parts + g],
                        a_buf.at[side, :, start : start + widths[g]],
                        a_sem.at[side, t * parts + g],
                    )
                )
    for copy in copies:
        copy.start()
    for e in range(chips):
        for t in range(planes):
            pltpu.make_async_copy(
                weights[e * planes + t],
                w_buf.at[e, :, t * block : (t + 1) * block],
                w_sem.at[e, t],
            ).start()
        if not e:
            for copy in more:
                copy.start()
    for copy in copies:
        copy.wait()


def weights_landed(planes, block, w_buf, w_sem, e):
    for t in range(planes):
        landed = w_buf.at[e, :, t * block : (t + 1) * block]
        pltpu.make_async_copy(landed, landed, w_sem.at[e, t]).wait()


def project_kernel(planes, widths, chips, *refs):
    pieces = planes * len(widths)
    where_ref, refs = refs[0], refs[1:]
    sides, refs = (refs[:pieces], refs[pieces : 2 * pieces]), refs[2 * pieces :]
    weights, refs = refs[: planes * chips], refs[planes * chips :]
    res, refs = refs[:planes], refs[planes:]
    gain, refs = refs[0], refs[1:]
    h_outs, refs = refs[:planes], refs[planes:]
    h_flip, sums, a_buf, w_buf, r_buf, h_buf, a_sem, w_sem, r_sem, h_sem = refs
    rows = a_buf.shape[1]
    chip = where_ref[0]
    plane = where_ref[1]
    more = [pltpu.make_async_copy(res[r], r_buf.at[r], r_sem.at[r]) for r in range(planes)]
    fill(planes, widths, sides, weights, a_buf, w_buf, a_sem, w_sem, more)
    for copy in more:
        copy.wait()
    sums[...] = jnp.zeros_like(sums)

    @pl.loop(0, chips)
    def _(e):
        weights_landed(planes, sum(widths), w_buf, w_sem, e)
        home = jnp.bitwise_xor(chip, e)
        gain_col = gain[home]
        came = lax.rem(plane - home + planes, planes)
        goes = lax.rem(home - plane + planes, planes)
        for side in range(2):
            total = dot_t(a_buf[side], w_buf[e])
            h = (r_buf[came, side].astype(F32) + total).astype(BF)
            h_buf[e, side] = h
            flip = h.astype(F32).T
            h_flip[e, :, side * rows : (side + 1) * rows] = flip.astype(BF)
            sums[2 * side : 2 * side + 1, :] += jnp.sum(flip * flip, 0, keepdims=True)
            sums[2 * side + 1 : 2 * side + 2, :] += jnp.sum(flip * gain_col, 0, keepdims=True)
        for r in range(planes):

            @pl.when(goes == r)
            def _(r=r):
                pltpu.make_async_copy(h_buf.at[e], h_outs[r], h_sem.at[r]).start()

    for r in range(planes):
        pltpu.make_async_copy(h_buf.at[0], h_outs[r], h_sem.at[r]).wait()


def project(where, own, other, weights, res, gain):
    planes = len(own)
    widths = tuple(a.shape[1] for a in own[0])
    chips = len(weights) // planes
    rows = own[0][0].shape[0]
    features = weights[0].shape[0]
    depth = planes * sum(widths)
    shape = jax.ShapeDtypeStruct
    any_spec = pl.BlockSpec(memory_space=pl.ANY)
    vmem_spec = pl.BlockSpec(memory_space=pltpu.VMEM)
    own, other = sum(own, []), sum(other, [])
    buffers = [pltpu.VMEM((2, rows, depth), BF), pltpu.VMEM((chips, features, depth), BF)]
    semaphores = [pltpu.SemaphoreType.DMA((2, len(own))), pltpu.SemaphoreType.DMA((chips, planes))]
    params = pltpu.CompilerParams(vmem_limit_bytes=VMEM_LIMIT)
    cost = pl.CostEstimate(
        flops=4 * rows * features * chips * depth, bytes_accessed=16 * 1024 * 1024, transcendentals=0
    )
    return pl.pallas_call(
        functools.partial(project_kernel, planes, widths, chips),
        out_shape=(
            *(shape((2, rows, features), BF),) * planes,
            shape((chips, features, 2 * rows), BF),
            shape((8, rows), F32),
        ),
        in_specs=[pl.BlockSpec(memory_space=pltpu.SMEM)]
        + [any_spec] * (2 * len(own) + planes * chips + planes)
        + [vmem_spec],
        out_specs=(any_spec,) * planes + (vmem_spec,) * 2,
        scratch_shapes=buffers
        + [
            pltpu.VMEM((planes, 2, rows, features), BF),
            pltpu.VMEM((chips, 2, rows, features), BF),
        ]
        + semaphores
        + [pltpu.SemaphoreType.DMA((n,)) for n in (planes, planes)],
        compiler_params=params,
        cost_estimate=cost,
        name="project",
    )(where, *own, *other, *weights, *res, gain)


def gradient_kernel(parts, order, *refs):
    grad = refs[0]
    own = refs[1 : 1 + parts]
    other = refs[1 + parts : 1 + 2 * parts]
    outs = refs[1 + 2 * parts :]
    rows = own[0].shape[0]
    count = len(order) // 2
    step = order[count]
    for out, base in zip(outs, (step, 0)):

        @pl.loop(0, count)
        def _(i):
            e = base + chip_index(order, i)
            start = 0
            for a, b in zip(own, other):
                total = dot(grad[e, :, :rows], a[...]) + dot(grad[e, :, rows:], b[...])
                out[i, :, start : start + a.shape[1]] = total.astype(BF)
                start += a.shape[1]


def chip_index(order, i):
    value = 0
    bit = 1
    while bit < len(order) // 2:
        value = value + jnp.where(jnp.bitwise_and(i, bit) != 0, order[bit], 0)
        bit *= 2
    return value


def gradient(grad, own, other, order):
    chips, features, tokens = grad.shape
    parts = len(own)
    width = sum(a.shape[1] for a in own)
    vmem_spec = pl.BlockSpec(memory_space=pltpu.VMEM)
    return pl.pallas_call(
        functools.partial(gradient_kernel, parts, order),
        out_shape=(jax.ShapeDtypeStruct((chips // 2, features, width), BF),) * 2,
        in_specs=[vmem_spec] * (1 + 2 * parts),
        out_specs=(vmem_spec,) * 2,
        compiler_params=pltpu.CompilerParams(vmem_limit_bytes=VMEM_LIMIT),
        cost_estimate=pl.CostEstimate(
            flops=2 * chips * features * tokens * width, bytes_accessed=8 * 1024 * 1024, transcendentals=0
        ),
        name="gradient",
    )(grad, *own, *other)


def place_kernel(count, axis, size, *refs):
    where_ref = refs[0]
    out = refs[-1]
    for i in range(count):
        start = pl.multiple_of(where_ref[i] * size, size)
        piece = refs[1 + i][...].astype(out.dtype)
        if axis == 0:
            out[pl.ds(start, size), :] = piece
        else:
            out[:, pl.ds(start, size)] = piece


def place(slots, pieces, axis, dtype):
    shape = list(pieces[0].shape)
    size = shape[axis]
    if axis == 1 and size % HD:
        order = jnp.argsort(slots)
        stacked = jnp.take(jnp.stack(pieces, 0), order, axis=0, mode="clip")
        return jnp.concatenate([stacked[i] for i in range(len(pieces))], 1).astype(dtype)
    shape[axis] *= len(pieces)
    vmem_spec = pl.BlockSpec(memory_space=pltpu.VMEM)
    return pl.pallas_call(
        functools.partial(place_kernel, len(pieces), axis, size),
        out_shape=jax.ShapeDtypeStruct(tuple(shape), dtype),
        in_specs=[pl.BlockSpec(memory_space=pltpu.SMEM)] + [vmem_spec] * len(pieces),
        out_specs=vmem_spec,
        compiler_params=pltpu.CompilerParams(vmem_limit_bytes=VMEM_LIMIT),
        cost_estimate=pl.CostEstimate(flops=0, bytes_accessed=6 * 1024 * 1024, transcendentals=0),
        name="place",
    )(slots.astype(jnp.int32), *pieces)


def place_rows_kernel(count, *refs):
    where_ref, pieces = refs[0], refs[1 : 1 + count]
    out, wide, sem = refs[-3:]
    size = wide.shape[1]
    copies = []
    for i in range(count):
        wide[i] = pieces[i][...].astype(F32)
        start = pl.multiple_of(where_ref[i] * size, size)
        copies.append(pltpu.make_async_copy(wide.at[i], out.at[pl.ds(start, size), :], sem.at[i]))
        copies[-1].start()
    for copy in copies:
        copy.wait()


def place_rows(slots, pieces, shape, before=None):
    count = len(pieces)
    extra = [] if before is None else [before]
    any_spec = pl.BlockSpec(memory_space=pl.ANY)
    return pl.pallas_call(
        functools.partial(place_rows_kernel, count),
        out_shape=jax.ShapeDtypeStruct(shape, F32),
        in_specs=[pl.BlockSpec(memory_space=pltpu.SMEM)]
        + [pl.BlockSpec(memory_space=pltpu.VMEM)] * count
        + [any_spec] * len(extra),
        out_specs=any_spec,
        scratch_shapes=[pltpu.VMEM((count, *pieces[0].shape), F32), pltpu.SemaphoreType.DMA((count,))],
        input_output_aliases={1 + count: 0} if extra else {},
        compiler_params=pltpu.CompilerParams(vmem_limit_bytes=VMEM_LIMIT),
        cost_estimate=pl.CostEstimate(flops=0, bytes_accessed=count * 1572864, transcendentals=0),
        name="place_rows",
    )(slots.astype(jnp.int32), *pieces, *extra)


def local(n_seq, n_head, prefix_k, prefix_v, queries, suffix_k, suffix_v, residual, out_weight,
          norm_gain, value_weight, prompt_of, suffix_len, return_table, return_index):
    chips = n_seq // 2
    bits = [1 << b for b in range(chips.bit_length() - 1)]
    rows = queries.shape[0]
    local_width = residual.shape[1]
    model = local_width * n_head
    kv_heads = prefix_k.shape[2] // HD
    group = queries.shape[1] // (kv_heads * HD)
    positions = prefix_k.shape[1]
    block_len = positions // n_seq
    seq = lax.axis_index("seq")
    plane = lax.axis_index("head")
    chip, core = seq // 2, seq % 2

    def seq_send(x, mask):
        return lax.ppermute(x, "seq", xor_perm(n_seq, mask))

    def partner(x):
        return seq_send(x, 1)

    def chip_send(x, bit):
        return seq_send(x, 2 * bit)

    def plane_send(x, step):
        return lax.ppermute(x, "head", shift_perm(n_head, step))

    def next_plane(step):
        return (plane + step) % n_head

    def plane_send(x, step):
        return lax.ppermute(x, "head", shift_perm(n_head, step))

    def next_plane(step):
        return (plane + step) % n_head

    weight_rows = out_weight.shape[0] // n_head
    w_own = []
    for t in range(n_head):
        piece = lax.dynamic_slice_in_dim(out_weight, next_plane(t) * weight_rows, weight_rows, 0)
        w_own.append(plane_send(piece, t) if t else piece)

    res = residual.reshape(rows, 2, n_head, weight_rows)
    mine = lax.dynamic_index_in_dim(res, core, 1, keepdims=False)
    yours = lax.dynamic_index_in_dim(res, 1 - core, 1, keepdims=False)
    theirs = partner(yours)
    res = []
    for t in range(n_head):
        piece = jnp.stack(
            [lax.dynamic_index_in_dim(x, next_plane(t), 1, keepdims=False) for x in (mine, theirs)], 0
        )
        res.append(plane_send(piece, t) if t else piece)

    gain_weight = norm_gain * value_weight
    gain = gain_weight.reshape(chips, 2, n_head, weight_rows)
    gain = lax.dynamic_index_in_dim(gain, core, 1, keepdims=False)
    gain = lax.dynamic_index_in_dim(gain, plane, 1, keepdims=False)

    bins = return_table.shape[0]
    one_hot = return_index[:, None] == jnp.arange(bins)[None, :]
    target = jnp.sum(jnp.where(one_hot, return_table[None, :], 0.0), 1)
    target_other = partner(target)

    pick = prompt_of.astype(jnp.int32)
    attn = []
    caches = ()
    for head in range(kv_heads):
        cut = slice(head * HD, (head + 1) * HD)
        both = jnp.stack([x[0, :, cut].reshape(n_seq, block_len, HD) for x in (prefix_k, prefix_v)], 1)
        if head:
            both = tie(both, kv)
        came = lax.all_to_all(both, "seq", split_axis=0, concat_axis=0, tiled=True)
        if head:
            came = tie(came, attn[-1])
        chosen, caches = route(pick, came, head, kv_heads, caches)
        kv = lax.all_to_all(chosen, "seq", split_axis=0, concat_axis=0, tiled=True)
        last = head == kv_heads - 1
        count = max(group // 2, 1) if last else group
        for step, first in enumerate(range(0, group, count)):
            if last and first + count == group:
                kv, *res = lax.optimization_barrier((kv, *res))
            attn.append(attention(queries, kv, suffix_k, suffix_v, head, group, first, count))
    cache_k, cache_v = caches

    half = n_head // 2
    w_own = list(lax.optimization_barrier((*w_own, attn[0]))[:-1])
    w_late = list(lax.optimization_barrier((*w_own, chosen))[:-1])
    weights = [w_own] + [None] * (chips - 1)
    for e in sorted(range(1, chips), key=lambda v: bin(v).count("1")):
        low, high = e & -e, 1 << (e.bit_length() - 1)
        got = [None] * n_head
        turn = [*range(half, n_head), *range(half)] if low == 1 else [*range(n_head)]
        for k, t in enumerate(turn):
            if low == high:
                got[t] = chip_send((w_late if k else w_own)[t], e)
            else:
                bit = low if t < half else high
                got[t] = chip_send(weights[e ^ bit][t], bit)
        weights[e] = got

    parts = len(attn)
    own = [[None] * parts for _ in range(n_head)]
    other = [[None] * parts for _ in range(n_head)]
    for g in range(parts):
        for t in range(n_head):
            if not t:
                own[t][g] = attn[g]
            elif g + 2 < parts or parts == 3 and not g:
                own[t][g] = plane_send(own[t - 1][g], 1)
            else:
                own[t][g] = plane_send(attn[g], t)
            other[t][g] = partner(own[t][g])

    where = jnp.stack([chip, plane]).astype(jnp.int32)
    weights = sum(weights, [])
    *h_outs, h_flip, sums = project(where, own, other, weights, res, gain[:, :, None])

    back = []
    for t in range(n_head):
        back.append(plane_send(h_outs[t], t) if t else h_outs[0])
    rest = partner(jnp.stack([piece[1] for piece in back], 0))
    pieces = [piece[0] for piece in back] + list(rest)
    slots = [side * n_head + next_plane(-t) for side in (core, 1 - core) for t in range(n_head)]
    hidden = place(jnp.stack(slots), pieces, 1, BF)

    yours = partner(sums[:4])
    totals = sums[:4] + jnp.concatenate([yours[2:], yours[:2]], 0)
    step = 1
    while step < n_head:
        totals = totals + lax.ppermute(totals, "head", xor_perm(n_head, step))
        step *= 2
    square_sum = jnp.concatenate([totals[0], totals[2]])
    weighted_sum = jnp.concatenate([totals[1], totals[3]])
    inverse = lax.rsqrt(square_sum / model + EPSILON)
    value_rows = weighted_sum * inverse
    targets = jnp.concatenate([target, target_other])
    position = jnp.arange(rows)
    live = jnp.concatenate([position < suffix_len[seq], position < suffix_len[seq ^ 1]])
    error = jnp.where(live, value_rows - targets, 0.0)
    first_term = error * inverse
    second_term = error * (weighted_sum * inverse * inverse * inverse) / model
    gain_near = jnp.take(gain, chip ^ jnp.arange(chips), axis=0, mode="clip")
    grad = (
        first_term[None, None, :] * gain_near[:, :, None] - second_term[None, None, :] * h_flip.astype(F32)
    ).astype(BF)

    final = []
    turns = sorted(range(n_head), key=lambda t: (t == 0, abs(2 * t - n_head), t))
    for t in turns:
        turn = bits if t % 2 else bits[::-1]
        order = [sum(bit for k, bit in enumerate(turn[::-1]) if i >> k & 1) for i in range(chips)]
        send, keep = gradient(grad, own[t], other[t], order)
        for bit in turn:
            got = chip_send(send, bit)
            half = keep.shape[0] // 2
            if half:
                send = (keep[half:].astype(F32) + got[half:].astype(F32)).astype(BF)
                keep = (keep[:half].astype(F32) + got[:half].astype(F32)).astype(BF)
            else:
                keep = (keep.astype(F32) + got.astype(F32)).astype(BF)
        final.append(plane_send(keep[0], -t) if t else keep[0])
    late = turns.index(n_head - 1)
    early = [i for i in range(n_head) if i != late]
    shape = (n_head * weight_rows, out_weight.shape[1])
    grad_out = place_rows(jnp.stack([next_plane(turns[i]) for i in early]), [final[i] for i in early], shape)
    grad_out = place_rows(next_plane(turns[late])[None], [final[late]], shape, grad_out)
    return (cache_k, cache_v, hidden, value_rows[:rows], grad_out)


def solution(mesh):
    in_specs = (
        P("seq", None, "head"),
        P("seq", None, "head"),
        P("seq", "head"),
        P("seq", "head"),
        P("seq", "head"),
        P("seq", "head"),
        P("seq", "head"),
        P(),
        P(),
        P(),
        P(),
        P(),
        P("seq"),
    )
    out_specs = (
        P(None, "seq", "head"),
        P(None, "seq", "head"),
        P("seq", "head"),
        P("seq"),
        P("seq", "head"),
    )
    body = functools.partial(local, mesh.shape["seq"], mesh.shape["head"])

    return jax.shard_map(body, mesh=mesh, in_specs=in_specs, out_specs=out_specs, check_vma=False)
```

```python
import functools
import math

import jax
import jax.numpy as jnp
from jax import lax
from jax.experimental import pallas as pl
from jax.experimental.pallas import tpu as pltpu
from jax.sharding import PartitionSpec as P


HD = 128
EPSILON = 1e-05
MASKED = -1e30
BF = jnp.bfloat16
F32 = jnp.float32
TILE = 256
VMEM_LIMIT = 60 * 1024 * 1024


def tie(x, *deps):
    return lax.optimization_barrier((x, *deps))[0]


def shift_perm(count, step):
    return [(i, (i + step) % count) for i in range(count)]


def xor_perm(count, mask):
    return [(i, i ^ mask) for i in range(count)]


def dot_t(a, b):
    return lax.dot_general(a, b, (((1,), (1,)), ((), ())), preferred_element_type=F32)


def dot(a, b):
    return lax.dot_general(a, b, (((1,), (0,)), ((), ())), preferred_element_type=F32)


def attention_kernel(q_ref, kv, sk_ref, sv_ref, o_ref, v_wide, scores):
    blocks = kv.shape[0]
    tile = q_ref.shape[0]
    block_len = kv.shape[2]
    own_len = sk_ref.shape[0]
    prefix_len = blocks * block_len
    scale = HD ** (-0.5) / math.log(2.0)

    @pl.when((pl.program_id(0) == 0) & (pl.program_id(1) == 0))
    def _():
        for b in range(blocks):
            v_wide[b * block_len : (b + 1) * block_len, :HD] = kv[b, 1]
        v_wide[prefix_len:, :HD] = sv_ref[...]
        v_wide[:, HD:] = jnp.ones((prefix_len + own_len, HD), BF)

    q = q_ref[...]
    spans = [(b * block_len, block_len) for b in range(blocks)]
    top = jnp.full((tile, HD), MASKED, F32)
    for b, (start, size) in enumerate(spans):
        s = dot_t(q, kv[b, 0])
        scores[:, start : start + size] = s
        for lane in range(0, size, HD):
            top = jnp.maximum(top, s[:, lane : lane + HD])
    s = dot_t(q, sk_ref[...])
    row = lax.broadcasted_iota(jnp.int32, (tile, own_len), 0) + pl.program_id(1) * tile
    col = lax.broadcasted_iota(jnp.int32, (tile, own_len), 1)
    s = jnp.where(col <= row, s, MASKED)
    scores[:, prefix_len:] = s
    for lane in range(0, own_len, HD):
        top = jnp.maximum(top, s[:, lane : lane + HD])
    row_max = jnp.max(top, 1, keepdims=True)
    mixed = jnp.zeros((tile, 2 * HD), F32)
    for start, size in spans + [(prefix_len, own_len)]:
        p = jnp.exp2((scores[:, start : start + size] - row_max) * scale)
        mixed = mixed + dot(p.astype(BF), v_wide[start : start + size, :])
    o_ref[...] = (mixed[:, :HD] / mixed[:, HD:]).astype(BF)


def attention(queries, kv, suffix_k, suffix_v, head, group, first, count):
    rows = queries.shape[0]
    tile = TILE
    blocks, _, block_len, _ = kv.shape
    span = blocks * block_len + rows
    return pl.pallas_call(
        attention_kernel,
        out_shape=jax.ShapeDtypeStruct((rows, count * HD), BF),
        grid=(count, rows // tile),
        in_specs=[pl.BlockSpec((tile, HD), lambda j, i: (i, head * group + first + j))]
        + [pl.BlockSpec(kv.shape, lambda j, i: (0, 0, 0, 0))]
        + [pl.BlockSpec((rows, HD), lambda j, i: (0, head))] * 2,
        out_specs=pl.BlockSpec((tile, HD), lambda j, i: (i, j)),
        scratch_shapes=[pltpu.VMEM((span, 2 * HD), BF), pltpu.VMEM((tile, span), F32)],
        compiler_params=pltpu.CompilerParams(vmem_limit_bytes=VMEM_LIMIT),
        cost_estimate=pl.CostEstimate(
            flops=4 * rows * count * span * HD, bytes_accessed=4 * span * HD, transcendentals=rows * count * span
        ),
        name="attend",
    )(queries, kv, suffix_k, suffix_v)


def route_kernel(head, *refs):
    pick, came = refs[:2]
    chosen, cache_k, cache_v, held, in_sem, out_sem, cache_sem = refs[-7:]
    count = held.shape[0]
    load = pltpu.make_async_copy(came, held, in_sem)
    load.start()
    load.wait()
    cut = pl.ds(head * HD, HD)
    copies = [pltpu.make_async_copy(held.at[pick[n]], chosen.at[n], out_sem.at[n]) for n in range(count)]
    for which, cache in enumerate((cache_k, cache_v)):
        copies.append(pltpu.make_async_copy(held.at[:, which], cache.at[:, :, cut], cache_sem.at[which]))
    for copy in copies:
        copy.start()
    for copy in copies:
        copy.wait()


def route(pick, came, head, kv_heads, caches):
    count, _, block_len, _ = came.shape
    cache = jax.ShapeDtypeStruct((count, block_len, kv_heads * HD), BF)
    any_spec = pl.BlockSpec(memory_space=pl.ANY)
    extra = list(caches)
    chosen, *caches = pl.pallas_call(
        functools.partial(route_kernel, head),
        out_shape=(jax.ShapeDtypeStruct(came.shape, BF), cache, cache),
        in_specs=[pl.BlockSpec(memory_space=pltpu.SMEM)] + [any_spec] * (1 + len(extra)),
        out_specs=(any_spec,) * 3,
        scratch_shapes=[
            pltpu.VMEM(came.shape, BF),
            pltpu.SemaphoreType.DMA,
            pltpu.SemaphoreType.DMA((count,)),
            pltpu.SemaphoreType.DMA((2,)),
        ],
        input_output_aliases={2: 1, 3: 2} if extra else {},
        compiler_params=pltpu.CompilerParams(vmem_limit_bytes=VMEM_LIMIT),
        cost_estimate=pl.CostEstimate(flops=0, bytes_accessed=8 * 1024 * 1024, transcendentals=0),
        name="route",
    )(pick, came, *extra)
    return chosen, caches


def fill(planes, widths, sides, weights, a_buf, w_buf, a_sem, w_sem, more):
    parts = len(widths)
    block = sum(widths)
    chips = len(weights) // planes
    copies = []
    for side in range(2):
        for t in range(planes):
            for g in range(parts):
                start = t * block + sum(widths[:g])
                copies.append(
                    pltpu.make_async_copy(
                        sides[side][t * parts + g],
                        a_buf.at[side, :, start : start + widths[g]],
                        a_sem.at[side, t * parts + g],
                    )
                )
    for copy in copies:
        copy.start()
    for e in range(chips):
        for t in range(planes):
            pltpu.make_async_copy(
                weights[e * planes + t],
                w_buf.at[e, :, t * block : (t + 1) * block],
                w_sem.at[e, t],
            ).start()
        if not e:
            for copy in more:
                copy.start()
    for copy in copies:
        copy.wait()


def weights_landed(planes, block, w_buf, w_sem, e):
    for t in range(planes):
        landed = w_buf.at[e, :, t * block : (t + 1) * block]
        pltpu.make_async_copy(landed, landed, w_sem.at[e, t]).wait()


def project_kernel(planes, widths, chips, sends, *refs):
    pieces = planes * len(widths)
    where_ref, refs = refs[0], refs[1:]
    sides, refs = (refs[:pieces], refs[pieces : 2 * pieces]), refs[2 * pieces :]
    weights, refs = refs[: planes * chips], refs[planes * chips :]
    res, refs = refs[:planes], refs[planes:]
    gain, refs = refs[0], refs[1:]
    h_outs, refs = refs[:planes], refs[planes:]
    flips, refs = refs[: len(sends)], refs[len(sends) :]
    h_flip, sums, a_buf, w_buf, r_buf, h_buf, a_sem, w_sem, r_sem, h_sem, f_sem = refs
    rows = a_buf.shape[1]
    chip = where_ref[0]
    plane = where_ref[1]
    more = [pltpu.make_async_copy(res[r], r_buf.at[r], r_sem.at[r]) for r in range(planes)]
    fill(planes, widths, sides, weights, a_buf, w_buf, a_sem, w_sem, more)
    for copy in more:
        copy.wait()
    sums[...] = jnp.zeros_like(sums)

    @pl.loop(0, chips)
    def _(e):
        weights_landed(planes, sum(widths), w_buf, w_sem, e)
        home = jnp.bitwise_xor(chip, e)
        gain_col = gain[home]
        came = lax.rem(plane - home + planes, planes)
        goes = lax.rem(home - plane + planes, planes)
        for side in range(2):
            total = dot_t(a_buf[side], w_buf[e])
            h = (r_buf[came, side].astype(F32) + total).astype(BF)
            h_buf[e, side] = h
            flip = h.astype(F32).T
            h_flip[e, :, side * rows : (side + 1) * rows] = flip.astype(BF)
            sums[2 * side : 2 * side + 1, :] += jnp.sum(flip * flip, 0, keepdims=True)
            sums[2 * side + 1 : 2 * side + 2, :] += jnp.sum(flip * gain_col, 0, keepdims=True)
        for r in range(planes):

            @pl.when(goes == r)
            def _(r=r):
                pltpu.make_async_copy(h_buf.at[e], h_outs[r], h_sem.at[r]).start()

        for j, chosen in enumerate(sends):
            for i, value in enumerate(chosen):

                @pl.when(e == value)
                def _(j=j, i=i):
                    pltpu.make_async_copy(h_flip.at[e], flips[j].at[i], f_sem.at[j, i]).start()

    for r in range(planes):
        pltpu.make_async_copy(h_buf.at[0], h_outs[r], h_sem.at[r]).wait()
    for j, chosen in enumerate(sends):
        for i in range(len(chosen)):
            pltpu.make_async_copy(h_flip.at[0], flips[j].at[i], f_sem.at[j, i]).wait()


def project(where, own, other, weights, res, gain, sends):
    planes = len(own)
    widths = tuple(a.shape[1] for a in own[0])
    chips = len(weights) // planes
    rows = own[0][0].shape[0]
    features = weights[0].shape[0]
    depth = planes * sum(widths)
    shape = jax.ShapeDtypeStruct
    any_spec = pl.BlockSpec(memory_space=pl.ANY)
    vmem_spec = pl.BlockSpec(memory_space=pltpu.VMEM)
    own, other = sum(own, []), sum(other, [])
    buffers = [pltpu.VMEM((2, rows, depth), BF), pltpu.VMEM((chips, features, depth), BF)]
    semaphores = [pltpu.SemaphoreType.DMA((2, len(own))), pltpu.SemaphoreType.DMA((chips, planes))]
    params = pltpu.CompilerParams(vmem_limit_bytes=VMEM_LIMIT)
    cost = pl.CostEstimate(
        flops=4 * rows * features * chips * depth, bytes_accessed=16 * 1024 * 1024, transcendentals=0
    )
    return pl.pallas_call(
        functools.partial(project_kernel, planes, widths, chips, sends),
        out_shape=(
            *(shape((2, rows, features), BF),) * planes,
            *(shape((len(chosen), features, 2 * rows), BF) for chosen in sends),
            shape((chips, features, 2 * rows), BF),
            shape((8, rows), F32),
        ),
        in_specs=[pl.BlockSpec(memory_space=pltpu.SMEM)]
        + [any_spec] * (2 * len(own) + planes * chips + planes)
        + [vmem_spec],
        out_specs=(any_spec,) * (planes + len(sends)) + (vmem_spec,) * 2,
        scratch_shapes=buffers
        + [
            pltpu.VMEM((planes, 2, rows, features), BF),
            pltpu.VMEM((chips, 2, rows, features), BF),
        ]
        + semaphores
        + [pltpu.SemaphoreType.DMA((n,)) for n in (planes, planes)]
        + [pltpu.SemaphoreType.DMA((max(len(sends), 1), 2))],
        compiler_params=params,
        cost_estimate=cost,
        name="project",
    )(where, *own, *other, *weights, *res, gain)


def gradient_kernel(parts, order, *refs):
    grad = refs[0]
    own = refs[1 : 1 + parts]
    other = refs[1 + parts : 1 + 2 * parts]
    outs = refs[1 + 2 * parts :]
    rows = own[0].shape[0]
    count = len(order) // 2
    step = order[count]
    for out, base in zip(outs, (step, 0)):

        @pl.loop(0, count)
        def _(i):
            e = base + chip_index(order, i)
            start = 0
            for a, b in zip(own, other):
                total = dot(grad[e, :, :rows], a[...]) + dot(grad[e, :, rows:], b[...])
                out[i, :, start : start + a.shape[1]] = total.astype(BF)
                start += a.shape[1]


def chip_index(order, i):
    value = 0
    bit = 1
    while bit < len(order) // 2:
        value = value + jnp.where(jnp.bitwise_and(i, bit) != 0, order[bit], 0)
        bit *= 2
    return value


def gradient(grad, own, other, order):
    chips, features, tokens = grad.shape
    parts = len(own)
    width = sum(a.shape[1] for a in own)
    vmem_spec = pl.BlockSpec(memory_space=pltpu.VMEM)
    return pl.pallas_call(
        functools.partial(gradient_kernel, parts, order),
        out_shape=(jax.ShapeDtypeStruct((chips // 2, features, width), BF),) * 2,
        in_specs=[vmem_spec] * (1 + 2 * parts),
        out_specs=(vmem_spec,) * 2,
        compiler_params=pltpu.CompilerParams(vmem_limit_bytes=VMEM_LIMIT),
        cost_estimate=pl.CostEstimate(
            flops=2 * chips * features * tokens * width, bytes_accessed=8 * 1024 * 1024, transcendentals=0
        ),
        name="gradient",
    )(grad, *own, *other)


def joint_kernel(parts, rest, *refs):
    grad, near = refs[:2]
    pieces, outs = refs[2 : 2 + 4 * parts], refs[2 + 4 * parts :]
    rows = pieces[0].shape[0]
    for out, e, i in ((outs[0], rest, 1), (outs[1], 0, 0)):
        start = 0
        for g in range(parts):
            own, other, near_own, near_other = (pieces[k * parts + g] for k in range(4))
            total = dot(grad[e, :, :rows], own[...]) + dot(grad[e, :, rows:], other[...])
            total += dot(near[i, :, :rows], near_own[...]) + dot(near[i, :, rows:], near_other[...])
            out[0, :, start : start + own.shape[1]] = total.astype(BF)
            start += own.shape[1]


def joint_gradient(grad, near, pieces, rest):
    chips, features, tokens = grad.shape
    width = sum(a.shape[1] for a in pieces[0])
    vmem_spec = pl.BlockSpec(memory_space=pltpu.VMEM)
    return pl.pallas_call(
        functools.partial(joint_kernel, len(pieces[0]), rest),
        out_shape=(jax.ShapeDtypeStruct((1, features, width), BF),) * 2,
        in_specs=[vmem_spec] * (2 + 4 * len(pieces[0])),
        out_specs=(vmem_spec,) * 2,
        compiler_params=pltpu.CompilerParams(vmem_limit_bytes=VMEM_LIMIT),
        cost_estimate=pl.CostEstimate(
            flops=2 * chips * features * tokens * width, bytes_accessed=8 * 1024 * 1024, transcendentals=0
        ),
        name="joint",
    )(grad, near, *sum(pieces, []))


def place_columns_kernel(count, *refs):
    where_ref, out = refs[0], refs[-1]
    size = refs[1].shape[2]
    for i in range(count):
        start = pl.multiple_of(where_ref[i] * size, size)
        out[:, pl.ds(start, size)] = refs[1 + i][2 * i // count]


def place_columns(slots, front, rear):
    pieces = list(front) + list(rear)
    count = len(pieces)
    _, rows, size = pieces[0].shape
    if size % HD:
        flat = jnp.stack([p[2 * i // count] for i, p in enumerate(pieces)], 0)
        flat = jnp.take(flat, jnp.argsort(slots), axis=0, mode="clip")
        return jnp.concatenate([flat[i] for i in range(count)], 1)
    vmem_spec = pl.BlockSpec(memory_space=pltpu.VMEM)
    return pl.pallas_call(
        functools.partial(place_columns_kernel, count),
        out_shape=jax.ShapeDtypeStruct((rows, count * size), BF),
        in_specs=[pl.BlockSpec(memory_space=pltpu.SMEM)] + [vmem_spec] * count,
        out_specs=vmem_spec,
        compiler_params=pltpu.CompilerParams(vmem_limit_bytes=VMEM_LIMIT),
        cost_estimate=pl.CostEstimate(flops=0, bytes_accessed=6 * 1024 * 1024, transcendentals=0),
        name="place_columns",
    )(slots.astype(jnp.int32), *pieces)


def place_rows_kernel(count, *refs):
    where_ref, pieces = refs[0], refs[1 : 1 + count]
    out, wide, sem = refs[-3:]
    size = wide.shape[1]
    copies = []
    for i in range(count):
        wide[i] = pieces[i][...].astype(F32)
        start = pl.multiple_of(where_ref[i] * size, size)
        copies.append(pltpu.make_async_copy(wide.at[i], out.at[pl.ds(start, size), :], sem.at[i]))
        copies[-1].start()
    for copy in copies:
        copy.wait()


def place_rows(slots, pieces, shape, before=None):
    count = len(pieces)
    extra = [] if before is None else [before]
    any_spec = pl.BlockSpec(memory_space=pl.ANY)
    return pl.pallas_call(
        functools.partial(place_rows_kernel, count),
        out_shape=jax.ShapeDtypeStruct(shape, F32),
        in_specs=[pl.BlockSpec(memory_space=pltpu.SMEM)]
        + [pl.BlockSpec(memory_space=pltpu.VMEM)] * count
        + [any_spec] * len(extra),
        out_specs=any_spec,
        scratch_shapes=[pltpu.VMEM((count, *pieces[0].shape), F32), pltpu.SemaphoreType.DMA((count,))],
        input_output_aliases={1 + count: 0} if extra else {},
        compiler_params=pltpu.CompilerParams(vmem_limit_bytes=VMEM_LIMIT),
        cost_estimate=pl.CostEstimate(flops=0, bytes_accessed=count * 1572864, transcendentals=0),
        name="place_rows",
    )(slots.astype(jnp.int32), *pieces, *extra)


def local(n_seq, n_head, prefix_k, prefix_v, queries, suffix_k, suffix_v, residual, out_weight,
          norm_gain, value_weight, prompt_of, suffix_len, return_table, return_index):
    chips = n_seq // 2
    bits = [1 << b for b in range(chips.bit_length() - 1)]
    rows = queries.shape[0]
    local_width = residual.shape[1]
    model = local_width * n_head
    kv_heads = prefix_k.shape[2] // HD
    group = queries.shape[1] // (kv_heads * HD)
    positions = prefix_k.shape[1]
    block_len = positions // n_seq
    seq = lax.axis_index("seq")
    plane = lax.axis_index("head")
    chip, core = seq // 2, seq % 2

    def seq_send(x, mask):
        return lax.ppermute(x, "seq", xor_perm(n_seq, mask))

    def partner(x):
        return seq_send(x, 1)

    def chip_send(x, bit):
        return seq_send(x, 2 * bit)

    def plane_send(x, step):
        return lax.ppermute(x, "head", shift_perm(n_head, step))

    def next_plane(step):
        return (plane + step) % n_head

    def plane_send(x, step):
        return lax.ppermute(x, "head", shift_perm(n_head, step))

    def next_plane(step):
        return (plane + step) % n_head

    weight_rows = out_weight.shape[0] // n_head
    w_own = []
    for t in range(n_head):
        piece = lax.dynamic_slice_in_dim(out_weight, next_plane(t) * weight_rows, weight_rows, 0)
        w_own.append(plane_send(piece, t) if t else piece)

    res = residual.reshape(rows, 2, n_head, weight_rows)
    mine = lax.dynamic_index_in_dim(res, core, 1, keepdims=False)
    yours = lax.dynamic_index_in_dim(res, 1 - core, 1, keepdims=False)
    theirs = partner(yours)
    res = []
    for t in range(n_head):
        piece = jnp.stack(
            [lax.dynamic_index_in_dim(x, next_plane(t), 1, keepdims=False) for x in (mine, theirs)], 0
        )
        res.append(plane_send(piece, t) if t else piece)

    gain_weight = norm_gain * value_weight
    gain = gain_weight.reshape(chips, 2, n_head, weight_rows)
    gain = lax.dynamic_index_in_dim(gain, core, 1, keepdims=False)
    gain = lax.dynamic_index_in_dim(gain, plane, 1, keepdims=False)

    bins = return_table.shape[0]
    one_hot = return_index[:, None] == jnp.arange(bins)[None, :]
    target = jnp.sum(jnp.where(one_hot, return_table[None, :], 0.0), 1)
    target_other = partner(target)

    pick = prompt_of.astype(jnp.int32)
    attn = []
    caches = ()
    for head in range(kv_heads):
        cut = slice(head * HD, (head + 1) * HD)
        both = jnp.stack([x[0, :, cut].reshape(n_seq, block_len, HD) for x in (prefix_k, prefix_v)], 1)
        if head:
            both = tie(both, kv)
        came = lax.all_to_all(both, "seq", split_axis=0, concat_axis=0, tiled=True)
        if head:
            came = tie(came, attn[-1])
        chosen, caches = route(pick, came, head, kv_heads, caches)
        kv = lax.all_to_all(chosen, "seq", split_axis=0, concat_axis=0, tiled=True)
        last = head == kv_heads - 1
        count = max(group // 2, 1) if last else group
        for step, first in enumerate(range(0, group, count)):
            if last and first + count == group:
                kv, *res = lax.optimization_barrier((kv, *res))
            attn.append(attention(queries, kv, suffix_k, suffix_v, head, group, first, count))
    cache_k, cache_v = caches

    half = n_head // 2
    w_own = list(lax.optimization_barrier((*w_own, attn[0]))[:-1])
    w_late = list(lax.optimization_barrier((*w_own, chosen))[:-1])
    weights = [w_own] + [None] * (chips - 1)
    for e in sorted(range(1, chips), key=lambda v: bin(v).count("1")):
        low, high = e & -e, 1 << (e.bit_length() - 1)
        got = [None] * n_head
        turn = [*range(half, n_head), *range(half)] if low == 1 else [*range(n_head)]
        for k, t in enumerate(turn):
            if low == high:
                got[t] = chip_send((w_late if k else w_own)[t], e)
            else:
                bit = low if t < half else high
                got[t] = chip_send(weights[e ^ bit][t], bit)
        weights[e] = got

    parts = len(attn)
    own = [[None] * parts for _ in range(n_head)]
    other = [[None] * parts for _ in range(n_head)]
    for g in range(parts):
        for t in range(n_head):
            if not t:
                own[t][g] = attn[g]
            elif g + 2 < parts or parts == 3 and not g:
                own[t][g] = plane_send(own[t - 1][g], 1)
            else:
                own[t][g] = plane_send(attn[g], t)
            other[t][g] = partner(own[t][g])

    early = {1: bits[0], 2: bits[1]} if len(bits) == 2 and n_head == 4 else {}
    near_attn = {}
    for t, bit in early.items():
        mine, theirs = [], []
        for g in range(parts):
            mine.append(chip_send(own[t][g], bit))
            theirs.append(partner(mine[-1]))
        near_attn[t] = mine, theirs

    where = jnp.stack([chip, plane]).astype(jnp.int32)
    weights = sum(weights, [])
    sends = [(bit, sum(bits)) for bit in early.values()]
    *h_outs, h_flip, sums = project(where, own, other, weights, res, gain[:, :, None], sends)
    h_outs, flips = h_outs[:n_head], h_outs[n_head:]

    near_flip = {}
    for (t, bit), flip in zip(early.items(), flips):
        near_flip[t] = chip_send(flip, bit)

    back = []
    for t in range(n_head):
        back.append(plane_send(h_outs[t], t) if t else h_outs[0])
    rest = [partner(piece) for piece in back]
    slots = [side * n_head + next_plane(-t) for side in (core, 1 - core) for t in range(n_head)]
    hidden = place_columns(jnp.stack(slots), back, rest)

    yours = partner(sums[:4])
    totals = sums[:4] + jnp.concatenate([yours[2:], yours[:2]], 0)
    step = 1
    while step < n_head:
        totals = totals + lax.ppermute(totals, "head", xor_perm(n_head, step))
        step *= 2
    square_sum = jnp.concatenate([totals[0], totals[2]])
    weighted_sum = jnp.concatenate([totals[1], totals[3]])
    inverse = lax.rsqrt(square_sum / model + EPSILON)
    value_rows = weighted_sum * inverse
    targets = jnp.concatenate([target, target_other])
    position = jnp.arange(rows)
    live = jnp.concatenate([position < suffix_len[seq], position < suffix_len[seq ^ 1]])
    error = jnp.where(live, value_rows - targets, 0.0)
    first_term = error * inverse
    second_term = error * (weighted_sum * inverse * inverse * inverse) / model
    gain_near = jnp.take(gain, chip ^ jnp.arange(chips), axis=0, mode="clip")

    def hidden_grad(terms, gains, flip):
        return (
            terms[0][None, None, :] * gains[:, :, None] - terms[1][None, None, :] * flip.astype(F32)
        ).astype(BF)

    terms = jnp.stack([first_term, second_term], 0)
    grad = hidden_grad(terms, gain_near, h_flip)
    near_grad = {}
    for t, bit in early.items():
        near_terms = chip_send(terms, bit)
        gains = jnp.stack([gain_near[0], gain_near[sum(bits) ^ bit]], 0)
        near_grad[t] = hidden_grad(near_terms, gains, near_flip[t])

    final = []
    turns = sorted(range(n_head), key=lambda t: (t != 0, t not in early, -t))
    for t in turns:
        turn = bits if t % 2 else bits[::-1]
        order = [sum(bit for k, bit in enumerate(turn[::-1]) if i >> k & 1) for i in range(chips)]
        if t in early:
            pieces = [own[t], other[t], *near_attn[t]]
            send, keep = joint_gradient(grad, near_grad[t], pieces, turn[1])
        else:
            send, keep = gradient(grad, own[t], other[t], order)
        for stage, bit in enumerate(turn):
            if t in early and not stage:
                continue
            got = chip_send(send, bit)
            half = keep.shape[0] // 2
            if half:
                send = (keep[half:].astype(F32) + got[half:].astype(F32)).astype(BF)
                keep = (keep[:half].astype(F32) + got[:half].astype(F32)).astype(BF)
            else:
                keep = (keep.astype(F32) + got.astype(F32)).astype(BF)
        final.append(plane_send(keep[0], -t) if t else keep[0])
    late = turns.index(n_head - 1)
    early = [i for i in range(n_head) if i != late]
    shape = (n_head * weight_rows, out_weight.shape[1])
    grad_out = place_rows(jnp.stack([next_plane(turns[i]) for i in early]), [final[i] for i in early], shape)
    grad_out = place_rows(next_plane(turns[late])[None], [final[late]], shape, grad_out)
    return (cache_k, cache_v, hidden, value_rows[:rows], grad_out)


def solution(mesh):
    in_specs = (
        P("seq", None, "head"),
        P("seq", None, "head"),
        P("seq", "head"),
        P("seq", "head"),
        P("seq", "head"),
        P("seq", "head"),
        P("seq", "head"),
        P(),
        P(),
        P(),
        P(),
        P(),
        P("seq"),
    )
    out_specs = (
        P(None, "seq", "head"),
        P(None, "seq", "head"),
        P("seq", "head"),
        P("seq"),
        P("seq", "head"),
    )
    body = functools.partial(local, mesh.shape["seq"], mesh.shape["head"])

    return jax.shard_map(body, mesh=mesh, in_specs=in_specs, out_specs=out_specs, check_vma=False)
```

```python
import functools
import math

import jax
import jax.numpy as jnp
from jax import lax
from jax.experimental import pallas as pl
from jax.experimental.pallas import tpu as pltpu
from jax.sharding import PartitionSpec as P


HD = 128
SEQ, HEAD = "seq", "head"
EPSILON = 1e-05
MASKED = -1e30
BF = jnp.bfloat16
F32 = jnp.float32
TILE = 256
VMEM_LIMIT = 60 * 1024 * 1024


def tie(x, *deps):
    return lax.optimization_barrier((x, *deps))[0]


def shift_perm(count, step):
    return [(i, (i + step) % count) for i in range(count)]


def xor_perm(count, mask):
    return [(i, i ^ mask) for i in range(count)]


def dot_t(a, b):
    return lax.dot_general(a, b, (((1,), (1,)), ((), ())), preferred_element_type=F32)


def dot(a, b):
    return lax.dot_general(a, b, (((1,), (0,)), ((), ())), preferred_element_type=F32)


def attention_kernel(q_ref, kv, sk_ref, sv_ref, o_ref, v_wide, scores):
    blocks = kv.shape[0]
    tile = q_ref.shape[0]
    block_len = kv.shape[2]
    own_len = sk_ref.shape[0]
    prefix_len = blocks * block_len
    scale = HD ** (-0.5) / math.log(2.0)

    @pl.when((pl.program_id(0) == 0) & (pl.program_id(1) == 0))
    def _():
        for b in range(blocks):
            v_wide[b * block_len : (b + 1) * block_len, :HD] = kv[b, 1]
        v_wide[prefix_len:, :HD] = sv_ref[...]
        v_wide[:, HD:] = jnp.ones((prefix_len + own_len, HD), BF)

    q = q_ref[...]
    spans = [(b * block_len, block_len) for b in range(blocks)]
    top = jnp.full((tile, HD), MASKED, F32)
    for b, (start, size) in enumerate(spans):
        s = dot_t(q, kv[b, 0])
        scores[:, start : start + size] = s
        for lane in range(0, size, HD):
            top = jnp.maximum(top, s[:, lane : lane + HD])
    s = dot_t(q, sk_ref[...])
    row = lax.broadcasted_iota(jnp.int32, (tile, own_len), 0) + pl.program_id(1) * tile
    col = lax.broadcasted_iota(jnp.int32, (tile, own_len), 1)
    s = jnp.where(col <= row, s, MASKED)
    scores[:, prefix_len:] = s
    for lane in range(0, own_len, HD):
        top = jnp.maximum(top, s[:, lane : lane + HD])
    row_max = jnp.max(top, 1, keepdims=True)
    mixed = jnp.zeros((tile, 2 * HD), F32)
    for start, size in spans + [(prefix_len, own_len)]:
        p = jnp.exp2((scores[:, start : start + size] - row_max) * scale)
        mixed = mixed + dot(p.astype(BF), v_wide[start : start + size, :])
    o_ref[...] = (mixed[:, :HD] / mixed[:, HD:]).astype(BF)


def attention(queries, kv, suffix_k, suffix_v, head, group, first, count):
    rows = queries.shape[0]
    tile = TILE
    blocks, _, block_len, _ = kv.shape
    span = blocks * block_len + rows
    return pl.pallas_call(
        attention_kernel,
        out_shape=jax.ShapeDtypeStruct((rows, count * HD), BF),
        grid=(count, rows // tile),
        in_specs=[pl.BlockSpec((tile, HD), lambda j, i: (i, head * group + first + j))]
        + [pl.BlockSpec(kv.shape, lambda j, i: (0, 0, 0, 0))]
        + [pl.BlockSpec((rows, HD), lambda j, i: (0, head))] * 2,
        out_specs=pl.BlockSpec((tile, HD), lambda j, i: (i, j)),
        scratch_shapes=[pltpu.VMEM((span, 2 * HD), BF), pltpu.VMEM((tile, span), F32)],
        compiler_params=pltpu.CompilerParams(vmem_limit_bytes=VMEM_LIMIT),
        cost_estimate=pl.CostEstimate(
            flops=4 * rows * count * span * HD, bytes_accessed=4 * span * HD, transcendentals=rows * count * span
        ),
        name="attend",
    )(queries, kv, suffix_k, suffix_v)


def route_kernel(head, *refs):
    pick, came = refs[:2]
    chosen, cache_k, cache_v, held, in_sem, out_sem, cache_sem = refs[-7:]
    count = held.shape[0]
    load = pltpu.make_async_copy(came, held, in_sem)
    load.start()
    load.wait()
    cut = pl.ds(head * HD, HD)
    copies = [pltpu.make_async_copy(held.at[pick[n]], chosen.at[n], out_sem.at[n]) for n in range(count)]
    for which, cache in enumerate((cache_k, cache_v)):
        copies.append(pltpu.make_async_copy(held.at[:, which], cache.at[:, :, cut], cache_sem.at[which]))
    for copy in copies:
        copy.start()
    for copy in copies:
        copy.wait()


def route(pick, came, head, kv_heads, caches):
    count, _, block_len, _ = came.shape
    cache = jax.ShapeDtypeStruct((count, block_len, kv_heads * HD), BF)
    any_spec = pl.BlockSpec(memory_space=pl.ANY)
    extra = list(caches)
    chosen, *caches = pl.pallas_call(
        functools.partial(route_kernel, head),
        out_shape=(jax.ShapeDtypeStruct(came.shape, BF), cache, cache),
        in_specs=[pl.BlockSpec(memory_space=pltpu.SMEM)] + [any_spec] * (1 + len(extra)),
        out_specs=(any_spec,) * 3,
        scratch_shapes=[
            pltpu.VMEM(came.shape, BF),
            pltpu.SemaphoreType.DMA,
            pltpu.SemaphoreType.DMA((count,)),
            pltpu.SemaphoreType.DMA((2,)),
        ],
        input_output_aliases={2: 1, 3: 2} if extra else {},
        compiler_params=pltpu.CompilerParams(vmem_limit_bytes=VMEM_LIMIT),
        cost_estimate=pl.CostEstimate(flops=0, bytes_accessed=8 * 1024 * 1024, transcendentals=0),
        name="route",
    )(pick, came, *extra)
    return chosen, caches


def fill(planes, widths, sides, weights, a_buf, w_buf, a_sem, w_sem, more):
    parts = len(widths)
    block = sum(widths)
    chips = len(weights) // planes
    rows = a_buf.shape[0] // 2
    copies = []
    for side in range(2):
        for t in range(planes):
            for g in range(parts):
                start = t * block + sum(widths[:g])
                copies.append(
                    pltpu.make_async_copy(
                        sides[side][t * parts + g],
                        a_buf.at[pl.ds(side * rows, rows), start : start + widths[g]],
                        a_sem.at[side, t * parts + g],
                    )
                )
    for copy in copies:
        copy.start()
    for e in range(chips):
        for t in range(planes):
            pltpu.make_async_copy(
                weights[e * planes + t],
                w_buf.at[e, :, t * block : (t + 1) * block],
                w_sem.at[e, t],
            ).start()
        if not e:
            for copy in more:
                copy.start()
    for copy in copies:
        copy.wait()


def weights_landed(planes, block, w_buf, w_sem, e):
    for t in range(planes):
        landed = w_buf.at[e, :, t * block : (t + 1) * block]
        pltpu.make_async_copy(landed, landed, w_sem.at[e, t]).wait()


def project_kernel(planes, widths, chips, sends, *refs):
    pieces = planes * len(widths)
    where_ref, refs = refs[0], refs[1:]
    sides, refs = (refs[:pieces], refs[pieces : 2 * pieces]), refs[2 * pieces :]
    weights, refs = refs[: planes * chips], refs[planes * chips :]
    res, refs = refs[:planes], refs[planes:]
    gain, refs = refs[0], refs[1:]
    h_outs, refs = refs[:planes], refs[planes:]
    flips, refs = refs[: len(sends)], refs[len(sends) :]
    h_flip, sums, a_buf, w_buf, r_buf, h_buf, a_sem, w_sem, r_sem, h_sem, f_sem = refs
    rows = a_buf.shape[0] // 2
    chip = where_ref[0]
    plane = where_ref[1]
    more = [pltpu.make_async_copy(res[r], r_buf.at[r], r_sem.at[r]) for r in range(planes)]
    fill(planes, widths, sides, weights, a_buf, w_buf, a_sem, w_sem, more)
    for copy in more:
        copy.wait()
    sums[...] = jnp.zeros_like(sums)

    @pl.loop(0, chips)
    def _(e):
        weights_landed(planes, sum(widths), w_buf, w_sem, e)
        home = jnp.bitwise_xor(chip, e)
        gain_col = gain[home]
        came = lax.rem(plane - home + planes, planes)
        goes = lax.rem(home - plane + planes, planes)
        both = dot_t(a_buf[...], w_buf[e])
        for side in range(2):
            total = both[side * rows : (side + 1) * rows]
            h = (r_buf[came, side].astype(F32) + total).astype(BF)
            h_buf[e, side] = h
            flip = h.astype(F32).T
            h_flip[e, :, side * rows : (side + 1) * rows] = flip.astype(BF)
            sums[2 * side : 2 * side + 1, :] += jnp.sum(flip * flip, 0, keepdims=True)
            sums[2 * side + 1 : 2 * side + 2, :] += jnp.sum(flip * gain_col, 0, keepdims=True)
        for r in range(planes):

            @pl.when(goes == r)
            def _(r=r):
                pltpu.make_async_copy(h_buf.at[e], h_outs[r], h_sem.at[r]).start()

        for j, chosen in enumerate(sends):
            for i, value in enumerate(chosen):

                @pl.when(e == value)
                def _(j=j, i=i):
                    pltpu.make_async_copy(h_flip.at[e], flips[j].at[i], f_sem.at[j, i]).start()

    for r in range(planes):
        pltpu.make_async_copy(h_buf.at[0], h_outs[r], h_sem.at[r]).wait()
    for j, chosen in enumerate(sends):
        for i in range(len(chosen)):
            pltpu.make_async_copy(h_flip.at[0], flips[j].at[i], f_sem.at[j, i]).wait()


def project(where, own, other, weights, res, gain, sends):
    planes = len(own)
    widths = tuple(a.shape[1] for a in own[0])
    chips = len(weights) // planes
    rows = own[0][0].shape[0]
    features = weights[0].shape[0]
    depth = planes * sum(widths)
    shape = jax.ShapeDtypeStruct
    any_spec = pl.BlockSpec(memory_space=pl.ANY)
    vmem_spec = pl.BlockSpec(memory_space=pltpu.VMEM)
    own, other = sum(own, []), sum(other, [])
    buffers = [pltpu.VMEM((2 * rows, depth), BF), pltpu.VMEM((chips, features, depth), BF)]
    semaphores = [pltpu.SemaphoreType.DMA((2, len(own))), pltpu.SemaphoreType.DMA((chips, planes))]
    params = pltpu.CompilerParams(vmem_limit_bytes=VMEM_LIMIT)
    cost = pl.CostEstimate(
        flops=4 * rows * features * chips * depth, bytes_accessed=16 * 1024 * 1024, transcendentals=0
    )
    return pl.pallas_call(
        functools.partial(project_kernel, planes, widths, chips, sends),
        out_shape=(
            *(shape((2, rows, features), BF),) * planes,
            *(shape((len(chosen), features, 2 * rows), BF) for chosen in sends),
            shape((chips, features, 2 * rows), BF),
            shape((8, rows), F32),
        ),
        in_specs=[pl.BlockSpec(memory_space=pltpu.SMEM)]
        + [any_spec] * (2 * len(own) + planes * chips + planes)
        + [vmem_spec],
        out_specs=(any_spec,) * (planes + len(sends)) + (vmem_spec,) * 2,
        scratch_shapes=buffers
        + [
            pltpu.VMEM((planes, 2, rows, features), BF),
            pltpu.VMEM((chips, 2, rows, features), BF),
        ]
        + semaphores
        + [pltpu.SemaphoreType.DMA((n,)) for n in (planes, planes)]
        + [pltpu.SemaphoreType.DMA((max(len(sends), 1), 2))],
        compiler_params=params,
        cost_estimate=cost,
        name="project",
    )(where, *own, *other, *weights, *res, gain)


def gradient_kernel(parts, order, *refs):
    grad = refs[0]
    own = refs[1 : 1 + parts]
    other = refs[1 + parts : 1 + 2 * parts]
    outs = refs[1 + 2 * parts :]
    rows = own[0].shape[0]
    count = len(order) // 2
    step = order[count]
    for out, base in zip(outs, (step, 0)):

        @pl.loop(0, count)
        def _(i):
            e = base + chip_index(order, i)
            start = 0
            for a, b in zip(own, other):
                total = dot(grad[e, :, :rows], a[...]) + dot(grad[e, :, rows:], b[...])
                out[i, :, start : start + a.shape[1]] = total.astype(BF)
                start += a.shape[1]


def chip_index(order, i):
    value = 0
    bit = 1
    while bit < len(order) // 2:
        value = value + jnp.where(jnp.bitwise_and(i, bit) != 0, order[bit], 0)
        bit *= 2
    return value


def gradient(grad, own, other, order):
    chips, features, tokens = grad.shape
    parts = len(own)
    width = sum(a.shape[1] for a in own)
    vmem_spec = pl.BlockSpec(memory_space=pltpu.VMEM)
    return pl.pallas_call(
        functools.partial(gradient_kernel, parts, order),
        out_shape=(jax.ShapeDtypeStruct((chips // 2, features, width), BF),) * 2,
        in_specs=[vmem_spec] * (1 + 2 * parts),
        out_specs=(vmem_spec,) * 2,
        compiler_params=pltpu.CompilerParams(vmem_limit_bytes=VMEM_LIMIT),
        cost_estimate=pl.CostEstimate(
            flops=2 * chips * features * tokens * width, bytes_accessed=8 * 1024 * 1024, transcendentals=0
        ),
        name="gradient",
    )(grad, *own, *other)


def joint_kernel(parts, rest, *refs):
    grad, near = refs[:2]
    pieces, outs = refs[2 : 2 + 4 * parts], refs[2 + 4 * parts :]
    rows = pieces[0].shape[0]
    for out, e, i in ((outs[0], rest, 1), (outs[1], 0, 0)):
        start = 0
        for g in range(parts):
            own, other, near_own, near_other = (pieces[k * parts + g] for k in range(4))
            total = dot(grad[e, :, :rows], own[...]) + dot(grad[e, :, rows:], other[...])
            total += dot(near[i, :, :rows], near_own[...]) + dot(near[i, :, rows:], near_other[...])
            out[0, :, start : start + own.shape[1]] = total.astype(BF)
            start += own.shape[1]


def joint_gradient(grad, near, pieces, rest):
    chips, features, tokens = grad.shape
    width = sum(a.shape[1] for a in pieces[0])
    vmem_spec = pl.BlockSpec(memory_space=pltpu.VMEM)
    return pl.pallas_call(
        functools.partial(joint_kernel, len(pieces[0]), rest),
        out_shape=(jax.ShapeDtypeStruct((1, features, width), BF),) * 2,
        in_specs=[vmem_spec] * (2 + 4 * len(pieces[0])),
        out_specs=(vmem_spec,) * 2,
        compiler_params=pltpu.CompilerParams(vmem_limit_bytes=VMEM_LIMIT),
        cost_estimate=pl.CostEstimate(
            flops=2 * chips * features * tokens * width, bytes_accessed=8 * 1024 * 1024, transcendentals=0
        ),
        name="joint",
    )(grad, near, *sum(pieces, []))


def place_columns_kernel(count, *refs):
    where_ref, out = refs[0], refs[-1]
    size = refs[1].shape[2]
    for i in range(count):
        start = pl.multiple_of(where_ref[i] * size, size)
        out[:, pl.ds(start, size)] = refs[1 + i][2 * i // count]


def place_columns(slots, front, rear):
    pieces = list(front) + list(rear)
    count = len(pieces)
    _, rows, size = pieces[0].shape
    if size % HD:
        flat = jnp.stack([p[2 * i // count] for i, p in enumerate(pieces)], 0)
        flat = jnp.take(flat, jnp.argsort(slots), axis=0, mode="clip")
        return jnp.concatenate([flat[i] for i in range(count)], 1)
    vmem_spec = pl.BlockSpec(memory_space=pltpu.VMEM)
    return pl.pallas_call(
        functools.partial(place_columns_kernel, count),
        out_shape=jax.ShapeDtypeStruct((rows, count * size), BF),
        in_specs=[pl.BlockSpec(memory_space=pltpu.SMEM)] + [vmem_spec] * count,
        out_specs=vmem_spec,
        compiler_params=pltpu.CompilerParams(vmem_limit_bytes=VMEM_LIMIT),
        cost_estimate=pl.CostEstimate(flops=0, bytes_accessed=6 * 1024 * 1024, transcendentals=0),
        name="place_columns",
    )(slots.astype(jnp.int32), *pieces)


def place_rows_kernel(count, *refs):
    where_ref, pieces = refs[0], refs[1 : 1 + count]
    out, wide, sem = refs[-3:]
    size = wide.shape[1]
    copies = []
    for i in range(count):
        wide[i] = pieces[i][...].astype(F32)
        start = pl.multiple_of(where_ref[i] * size, size)
        copies.append(pltpu.make_async_copy(wide.at[i], out.at[pl.ds(start, size), :], sem.at[i]))
        copies[-1].start()
    for copy in copies:
        copy.wait()


def place_rows(slots, pieces, shape, before=None):
    count = len(pieces)
    extra = [] if before is None else [before]
    any_spec = pl.BlockSpec(memory_space=pl.ANY)
    return pl.pallas_call(
        functools.partial(place_rows_kernel, count),
        out_shape=jax.ShapeDtypeStruct(shape, F32),
        in_specs=[pl.BlockSpec(memory_space=pltpu.SMEM)]
        + [pl.BlockSpec(memory_space=pltpu.VMEM)] * count
        + [any_spec] * len(extra),
        out_specs=any_spec,
        scratch_shapes=[pltpu.VMEM((count, *pieces[0].shape), F32), pltpu.SemaphoreType.DMA((count,))],
        input_output_aliases={1 + count: 0} if extra else {},
        compiler_params=pltpu.CompilerParams(vmem_limit_bytes=VMEM_LIMIT),
        cost_estimate=pl.CostEstimate(flops=0, bytes_accessed=count * 1572864, transcendentals=0),
        name="place_rows",
    )(slots.astype(jnp.int32), *pieces, *extra)


def local(n_seq, n_head, prefix_k, prefix_v, queries, suffix_k, suffix_v, residual, out_weight,
          norm_gain, value_weight, prompt_of, suffix_len, return_table, return_index):
    chips = n_seq // 2
    bits = [1 << b for b in range(chips.bit_length() - 1)]
    rows = queries.shape[0]
    local_width = residual.shape[1]
    model = local_width * n_head
    kv_heads = prefix_k.shape[2] // HD
    group = queries.shape[1] // (kv_heads * HD)
    positions = prefix_k.shape[1]
    block_len = positions // n_seq
    seq = lax.axis_index(SEQ)
    plane = lax.axis_index(HEAD)
    chip, core = seq // 2, seq % 2

    def seq_send(x, mask):
        return lax.ppermute(x, SEQ, xor_perm(n_seq, mask))

    def partner(x):
        return seq_send(x, 1)

    def chip_send(x, bit):
        return seq_send(x, 2 * bit)

    def plane_send(x, step):
        return lax.ppermute(x, HEAD, shift_perm(n_head, step))

    def next_plane(step):
        return (plane + step) % n_head

    def plane_send(x, step):
        return lax.ppermute(x, HEAD, shift_perm(n_head, step))

    def next_plane(step):
        return (plane + step) % n_head

    weight_rows = out_weight.shape[0] // n_head
    w_own = []
    for t in range(n_head):
        piece = lax.dynamic_slice_in_dim(out_weight, next_plane(t) * weight_rows, weight_rows, 0)
        w_own.append(plane_send(piece, t) if t else piece)

    res = residual.reshape(rows, 2, n_head, weight_rows)
    mine = lax.dynamic_index_in_dim(res, core, 1, keepdims=False)
    yours = lax.dynamic_index_in_dim(res, 1 - core, 1, keepdims=False)
    theirs = partner(yours)
    res = []
    for t in range(n_head):
        piece = jnp.stack(
            [lax.dynamic_index_in_dim(x, next_plane(t), 1, keepdims=False) for x in (mine, theirs)], 0
        )
        res.append(plane_send(piece, t) if t else piece)

    gain_weight = norm_gain * value_weight
    gain = gain_weight.reshape(chips, 2, n_head, weight_rows)
    gain = lax.dynamic_index_in_dim(gain, core, 1, keepdims=False)
    gain = lax.dynamic_index_in_dim(gain, plane, 1, keepdims=False)

    bins = return_table.shape[0]
    one_hot = return_index[:, None] == jnp.arange(bins)[None, :]
    target = jnp.sum(jnp.where(one_hot, return_table[None, :], 0.0), 1)
    target_other = partner(target)

    pick = prompt_of.astype(jnp.int32)
    attn = []
    caches = ()
    for head in range(kv_heads):
        cut = slice(head * HD, (head + 1) * HD)
        both = jnp.stack([x[0, :, cut].reshape(n_seq, block_len, HD) for x in (prefix_k, prefix_v)], 1)
        if head:
            both = tie(both, kv)
        came = lax.all_to_all(both, SEQ, split_axis=0, concat_axis=0, tiled=True)
        if head:
            came = tie(came, attn[-1])
        chosen, caches = route(pick, came, head, kv_heads, caches)
        kv = lax.all_to_all(chosen, SEQ, split_axis=0, concat_axis=0, tiled=True)
        last = head == kv_heads - 1
        count = max(group // 2, 1) if last else group
        for step, first in enumerate(range(0, group, count)):
            if last and first + count == group:
                kv, *res = lax.optimization_barrier((kv, *res))
            attn.append(attention(queries, kv, suffix_k, suffix_v, head, group, first, count))
    cache_k, cache_v = caches

    half = n_head // 2
    w_own = list(lax.optimization_barrier((*w_own, attn[0]))[:-1])
    w_late = list(lax.optimization_barrier((*w_own, chosen))[:-1])
    weights = [w_own] + [None] * (chips - 1)
    for e in sorted(range(1, chips), key=lambda v: bin(v).count("1")):
        low, high = e & -e, 1 << (e.bit_length() - 1)
        got = [None] * n_head
        turn = [*range(half, n_head), *range(half)] if low == 1 else [*range(n_head)]
        for k, t in enumerate(turn):
            if low == high:
                got[t] = chip_send((w_late if k else w_own)[t], e)
            else:
                bit = low if t < half else high
                got[t] = chip_send(weights[e ^ bit][t], bit)
        weights[e] = got

    parts = len(attn)
    own = [[None] * parts for _ in range(n_head)]
    other = [[None] * parts for _ in range(n_head)]
    for g in range(parts):
        for t in range(n_head):
            if not t:
                own[t][g] = attn[g]
            elif g + 2 < parts or parts == 3 and not g:
                own[t][g] = plane_send(own[t - 1][g], 1)
            else:
                own[t][g] = plane_send(attn[g], t)
            other[t][g] = partner(own[t][g])

    early = {1: bits[0], 2: bits[1]} if len(bits) == 2 and n_head == 4 else {}
    near_attn = {}
    for t, bit in early.items():
        mine, theirs = [], []
        for g in range(parts):
            mine.append(chip_send(own[t][g], bit))
            theirs.append(partner(mine[-1]))
        near_attn[t] = mine, theirs

    where = jnp.stack([chip, plane]).astype(jnp.int32)
    weights = sum(weights, [])
    sends = [(bit, sum(bits)) for bit in early.values()]
    *h_outs, h_flip, sums = project(where, own, other, weights, res, gain[:, :, None], sends)
    h_outs, flips = h_outs[:n_head], h_outs[n_head:]

    near_flip = {}
    for (t, bit), flip in zip(early.items(), flips):
        near_flip[t] = chip_send(flip, bit)

    back = []
    for t in range(n_head):
        back.append(plane_send(h_outs[t], t) if t else h_outs[0])
    rest = [partner(piece) for piece in back]
    slots = [side * n_head + next_plane(-t) for side in (core, 1 - core) for t in range(n_head)]
    hidden = place_columns(jnp.stack(slots), back, rest)

    yours = partner(sums[:4])
    totals = sums[:4] + jnp.concatenate([yours[2:], yours[:2]], 0)
    step = 1
    while step < n_head:
        totals = totals + lax.ppermute(totals, HEAD, xor_perm(n_head, step))
        step *= 2
    square_sum = jnp.concatenate([totals[0], totals[2]])
    weighted_sum = jnp.concatenate([totals[1], totals[3]])
    inverse = lax.rsqrt(square_sum / model + EPSILON)
    value_rows = weighted_sum * inverse
    targets = jnp.concatenate([target, target_other])
    position = jnp.arange(rows)
    live = jnp.concatenate([position < suffix_len[seq], position < suffix_len[seq ^ 1]])
    error = jnp.where(live, value_rows - targets, 0.0)
    first_term = error * inverse
    second_term = error * (weighted_sum * inverse * inverse * inverse) / model
    gain_near = jnp.take(gain, chip ^ jnp.arange(chips), axis=0, mode="clip")

    def hidden_grad(terms, gains, flip):
        return (
            terms[0][None, None, :] * gains[:, :, None] - terms[1][None, None, :] * flip.astype(F32)
        ).astype(BF)

    terms = jnp.stack([first_term, second_term], 0)
    grad = hidden_grad(terms, gain_near, h_flip)
    near_grad = {}
    for t, bit in early.items():
        near_terms = chip_send(terms, bit)
        gains = jnp.stack([gain_near[0], gain_near[sum(bits) ^ bit]], 0)
        near_grad[t] = hidden_grad(near_terms, gains, near_flip[t])

    final = []
    turns = sorted(range(n_head), key=lambda t: (t != 0, t not in early, -t))
    for t in turns:
        turn = bits if t % 2 else bits[::-1]
        order = [sum(bit for k, bit in enumerate(turn[::-1]) if i >> k & 1) for i in range(chips)]
        if t in early:
            pieces = [own[t], other[t], *near_attn[t]]
            send, keep = joint_gradient(grad, near_grad[t], pieces, turn[1])
        else:
            send, keep = gradient(grad, own[t], other[t], order)
        for stage, bit in enumerate(turn):
            if t in early and not stage:
                continue
            got = chip_send(send, bit)
            half = keep.shape[0] // 2
            if half:
                send = (keep[half:].astype(F32) + got[half:].astype(F32)).astype(BF)
                keep = (keep[:half].astype(F32) + got[:half].astype(F32)).astype(BF)
            else:
                keep = (keep.astype(F32) + got.astype(F32)).astype(BF)
        final.append(plane_send(keep[0], -t) if t else keep[0])
    late = turns.index(n_head - 1)
    early = [i for i in range(n_head) if i != late]
    shape = (n_head * weight_rows, out_weight.shape[1])
    grad_out = place_rows(jnp.stack([next_plane(turns[i]) for i in early]), [final[i] for i in early], shape)
    grad_out = place_rows(next_plane(turns[late])[None], [final[late]], shape, grad_out)
    return (cache_k, cache_v, hidden, value_rows[:rows], grad_out)


def solution(mesh):
    in_specs = (
        P(SEQ, None, HEAD),
        P(SEQ, None, HEAD),
        P(SEQ, HEAD),
        P(SEQ, HEAD),
        P(SEQ, HEAD),
        P(SEQ, HEAD),
        P(SEQ, HEAD),
        P(),
        P(),
        P(),
        P(),
        P(),
        P(SEQ),
    )
    out_specs = (
        P(None, SEQ, HEAD),
        P(None, SEQ, HEAD),
        P(SEQ, HEAD),
        P(SEQ),
        P(SEQ, HEAD),
    )
    body = functools.partial(local, mesh.shape[SEQ], mesh.shape[HEAD])

    return jax.shard_map(body, mesh=mesh, in_specs=in_specs, out_specs=out_specs, check_vma=False)
```

```python
import functools
import math

import jax
import jax.numpy as jnp
from jax import lax
from jax.experimental import pallas as pl
from jax.experimental.pallas import tpu as pltpu
from jax.sharding import PartitionSpec as P


HD = 128
SEQ, HEAD = "seq", "head"
EPSILON = 1e-05
MASKED = -1e30
BF = jnp.bfloat16
F32 = jnp.float32
TILE = 256
VMEM_LIMIT = 60 * 1024 * 1024


def tie(x, *deps):
    return lax.optimization_barrier((x, *deps))[0]


def shift_perm(count, step):
    return [(i, (i + step) % count) for i in range(count)]


def xor_perm(count, mask):
    return [(i, i ^ mask) for i in range(count)]


def dot_t(a, b):
    return lax.dot_general(a, b, (((1,), (1,)), ((), ())), preferred_element_type=F32)


def dot(a, b):
    return lax.dot_general(a, b, (((1,), (0,)), ((), ())), preferred_element_type=F32)


def attention_kernel(q_ref, kv, sk_ref, sv_ref, o_ref, v_wide, scores):
    blocks = kv.shape[0]
    tile = q_ref.shape[0]
    block_len = kv.shape[2]
    own_len = sk_ref.shape[0]
    prefix_len = blocks * block_len
    scale = HD ** (-0.5) / math.log(2.0)

    @pl.when((pl.program_id(0) == 0) & (pl.program_id(1) == 0))
    def _():
        for b in range(blocks):
            v_wide[b * block_len : (b + 1) * block_len, :HD] = kv[b, 1]
        v_wide[prefix_len:, :HD] = sv_ref[...]
        v_wide[:, HD:] = jnp.ones((prefix_len + own_len, HD), BF)

    q = q_ref[...]
    spans = [(b * block_len, block_len) for b in range(blocks)]
    top = jnp.full((tile, HD), MASKED, F32)
    for b, (start, size) in enumerate(spans):
        s = dot_t(q, kv[b, 0])
        scores[:, start : start + size] = s
        for lane in range(0, size, HD):
            top = jnp.maximum(top, s[:, lane : lane + HD])
    s = dot_t(q, sk_ref[...])
    row = lax.broadcasted_iota(jnp.int32, (tile, own_len), 0) + pl.program_id(1) * tile
    col = lax.broadcasted_iota(jnp.int32, (tile, own_len), 1)
    s = jnp.where(col <= row, s, MASKED)
    scores[:, prefix_len:] = s
    for lane in range(0, own_len, HD):
        top = jnp.maximum(top, s[:, lane : lane + HD])
    row_max = jnp.max(top, 1, keepdims=True)
    mixed = jnp.zeros((tile, 2 * HD), F32)
    for start, size in spans + [(prefix_len, own_len)]:
        p = jnp.exp2((scores[:, start : start + size] - row_max) * scale)
        mixed = mixed + dot(p.astype(BF), v_wide[start : start + size, :])
    o_ref[...] = (mixed[:, :HD] / mixed[:, HD:]).astype(BF)


def attention(queries, kv, suffix_k, suffix_v, head, group, first, count, tile):
    rows = queries.shape[0]
    blocks, _, block_len, _ = kv.shape
    span = blocks * block_len + rows
    return pl.pallas_call(
        attention_kernel,
        out_shape=jax.ShapeDtypeStruct((rows, count * HD), BF),
        grid=(count, rows // tile),
        in_specs=[pl.BlockSpec((tile, HD), lambda j, i: (i, head * group + first + j))]
        + [pl.BlockSpec(kv.shape, lambda j, i: (0, 0, 0, 0))]
        + [pl.BlockSpec((rows, HD), lambda j, i: (0, head))] * 2,
        out_specs=pl.BlockSpec((tile, HD), lambda j, i: (i, j)),
        scratch_shapes=[pltpu.VMEM((span, 2 * HD), BF), pltpu.VMEM((tile, span), F32)],
        compiler_params=pltpu.CompilerParams(vmem_limit_bytes=VMEM_LIMIT),
        cost_estimate=pl.CostEstimate(
            flops=4 * rows * count * span * HD, bytes_accessed=4 * span * HD, transcendentals=rows * count * span
        ),
        name="attend",
    )(queries, kv, suffix_k, suffix_v)


def route_kernel(head, *refs):
    pick, came = refs[:2]
    chosen, cache_k, cache_v, held, in_sem, out_sem, cache_sem = refs[-7:]
    count = held.shape[0]
    load = pltpu.make_async_copy(came, held, in_sem)
    load.start()
    load.wait()
    cut = pl.ds(head * HD, HD)
    copies = [pltpu.make_async_copy(held.at[pick[n]], chosen.at[n], out_sem.at[n]) for n in range(count)]
    for which, cache in enumerate((cache_k, cache_v)):
        copies.append(pltpu.make_async_copy(held.at[:, which], cache.at[:, :, cut], cache_sem.at[which]))
    for copy in copies:
        copy.start()
    for copy in copies:
        copy.wait()


def route(pick, came, head, kv_heads, caches):
    count, _, block_len, _ = came.shape
    cache = jax.ShapeDtypeStruct((count, block_len, kv_heads * HD), BF)
    any_spec = pl.BlockSpec(memory_space=pl.ANY)
    extra = list(caches)
    chosen, *caches = pl.pallas_call(
        functools.partial(route_kernel, head),
        out_shape=(jax.ShapeDtypeStruct(came.shape, BF), cache, cache),
        in_specs=[pl.BlockSpec(memory_space=pltpu.SMEM)] + [any_spec] * (1 + len(extra)),
        out_specs=(any_spec,) * 3,
        scratch_shapes=[
            pltpu.VMEM(came.shape, BF),
            pltpu.SemaphoreType.DMA,
            pltpu.SemaphoreType.DMA((count,)),
            pltpu.SemaphoreType.DMA((2,)),
        ],
        input_output_aliases={2: 1, 3: 2} if extra else {},
        compiler_params=pltpu.CompilerParams(vmem_limit_bytes=VMEM_LIMIT),
        cost_estimate=pl.CostEstimate(flops=0, bytes_accessed=8 * 1024 * 1024, transcendentals=0),
        name="route",
    )(pick, came, *extra)
    return chosen, caches


def fill(planes, widths, sides, weights, a_buf, w_buf, a_sem, w_sem, more):
    parts = len(widths)
    block = sum(widths)
    chips = len(weights) // planes
    rows = a_buf.shape[0] // 2
    copies = []
    for side in range(2):
        for t in range(planes):
            for g in range(parts):
                start = t * block + sum(widths[:g])
                copies.append(
                    pltpu.make_async_copy(
                        sides[side][t * parts + g],
                        a_buf.at[pl.ds(side * rows, rows), start : start + widths[g]],
                        a_sem.at[side, t * parts + g],
                    )
                )
    for copy in copies:
        copy.start()
    for e in range(chips):
        for t in range(planes):
            pltpu.make_async_copy(
                weights[e * planes + t],
                w_buf.at[e, :, t * block : (t + 1) * block],
                w_sem.at[e, t],
            ).start()
        if not e:
            for copy in more:
                copy.start()
    for copy in copies:
        copy.wait()


def weights_landed(planes, block, w_buf, w_sem, e):
    for t in range(planes):
        landed = w_buf.at[e, :, t * block : (t + 1) * block]
        pltpu.make_async_copy(landed, landed, w_sem.at[e, t]).wait()


def project_kernel(planes, widths, chips, sends, *refs):
    pieces = planes * len(widths)
    where_ref, refs = refs[0], refs[1:]
    sides, refs = (refs[:pieces], refs[pieces : 2 * pieces]), refs[2 * pieces :]
    weights, refs = refs[: planes * chips], refs[planes * chips :]
    res, refs = refs[:planes], refs[planes:]
    gain, refs = refs[0], refs[1:]
    h_outs, refs = refs[:planes], refs[planes:]
    flips, refs = refs[: len(sends)], refs[len(sends) :]
    h_flip, sums, a_buf, w_buf, r_buf, h_buf, a_sem, w_sem, r_sem, h_sem, f_sem = refs
    rows = a_buf.shape[0] // 2
    chip = where_ref[0]
    plane = where_ref[1]
    more = [pltpu.make_async_copy(res[r], r_buf.at[r], r_sem.at[r]) for r in range(planes)]
    fill(planes, widths, sides, weights, a_buf, w_buf, a_sem, w_sem, more)
    for copy in more:
        copy.wait()
    sums[...] = jnp.zeros_like(sums)

    @pl.loop(0, chips)
    def _(e):
        weights_landed(planes, sum(widths), w_buf, w_sem, e)
        home = jnp.bitwise_xor(chip, e)
        gain_col = gain[home]
        came = lax.rem(plane - home + planes, planes)
        goes = lax.rem(home - plane + planes, planes)
        both = dot_t(a_buf[...], w_buf[e])
        for side in range(2):
            total = both[side * rows : (side + 1) * rows]
            h = (r_buf[came, side].astype(F32) + total).astype(BF)
            h_buf[e, side] = h
            flip = h.astype(F32).T
            h_flip[e, :, side * rows : (side + 1) * rows] = flip.astype(BF)
            sums[2 * side : 2 * side + 1, :] += jnp.sum(flip * flip, 0, keepdims=True)
            sums[2 * side + 1 : 2 * side + 2, :] += jnp.sum(flip * gain_col, 0, keepdims=True)
        for r in range(planes):

            @pl.when(goes == r)
            def _(r=r):
                pltpu.make_async_copy(h_buf.at[e], h_outs[r], h_sem.at[r]).start()

        for j, chosen in enumerate(sends):
            for i, value in enumerate(chosen):

                @pl.when(e == value)
                def _(j=j, i=i):
                    pltpu.make_async_copy(h_flip.at[e], flips[j].at[i], f_sem.at[j, i]).start()

    for r in range(planes):
        pltpu.make_async_copy(h_buf.at[0], h_outs[r], h_sem.at[r]).wait()
    for j, chosen in enumerate(sends):
        for i in range(len(chosen)):
            pltpu.make_async_copy(h_flip.at[0], flips[j].at[i], f_sem.at[j, i]).wait()


def project(where, own, other, weights, res, gain, sends):
    planes = len(own)
    widths = tuple(a.shape[1] for a in own[0])
    chips = len(weights) // planes
    rows = own[0][0].shape[0]
    features = weights[0].shape[0]
    depth = planes * sum(widths)
    shape = jax.ShapeDtypeStruct
    any_spec = pl.BlockSpec(memory_space=pl.ANY)
    vmem_spec = pl.BlockSpec(memory_space=pltpu.VMEM)
    own, other = sum(own, []), sum(other, [])
    buffers = [pltpu.VMEM((2 * rows, depth), BF), pltpu.VMEM((chips, features, depth), BF)]
    semaphores = [pltpu.SemaphoreType.DMA((2, len(own))), pltpu.SemaphoreType.DMA((chips, planes))]
    params = pltpu.CompilerParams(vmem_limit_bytes=VMEM_LIMIT)
    cost = pl.CostEstimate(
        flops=4 * rows * features * chips * depth, bytes_accessed=16 * 1024 * 1024, transcendentals=0
    )
    return pl.pallas_call(
        functools.partial(project_kernel, planes, widths, chips, sends),
        out_shape=(
            *(shape((2, rows, features), BF),) * planes,
            *(shape((len(chosen), features, 2 * rows), BF) for chosen in sends),
            shape((chips, features, 2 * rows), BF),
            shape((8, rows), F32),
        ),
        in_specs=[pl.BlockSpec(memory_space=pltpu.SMEM)]
        + [any_spec] * (2 * len(own) + planes * chips + planes)
        + [vmem_spec],
        out_specs=(any_spec,) * (planes + len(sends)) + (vmem_spec,) * 2,
        scratch_shapes=buffers
        + [
            pltpu.VMEM((planes, 2, rows, features), BF),
            pltpu.VMEM((chips, 2, rows, features), BF),
        ]
        + semaphores
        + [pltpu.SemaphoreType.DMA((n,)) for n in (planes, planes)]
        + [pltpu.SemaphoreType.DMA((max(len(sends), 1), 2))],
        compiler_params=params,
        cost_estimate=cost,
        name="project",
    )(where, *own, *other, *weights, *res, gain)


def gradient_kernel(parts, order, *refs):
    grad = refs[0]
    own = refs[1 : 1 + parts]
    other = refs[1 + parts : 1 + 2 * parts]
    outs = refs[1 + 2 * parts :]
    rows = own[0].shape[0]
    count = len(order) // 2
    step = order[count]
    for out, base in zip(outs, (step, 0)):

        @pl.loop(0, count)
        def _(i):
            e = base + chip_index(order, i)
            start = 0
            for a, b in zip(own, other):
                total = dot(grad[e, :, :rows], a[...]) + dot(grad[e, :, rows:], b[...])
                out[i, :, start : start + a.shape[1]] = total.astype(BF)
                start += a.shape[1]


def chip_index(order, i):
    value = 0
    bit = 1
    while bit < len(order) // 2:
        value = value + jnp.where(jnp.bitwise_and(i, bit) != 0, order[bit], 0)
        bit *= 2
    return value


def gradient(grad, own, other, order):
    chips, features, tokens = grad.shape
    parts = len(own)
    width = sum(a.shape[1] for a in own)
    vmem_spec = pl.BlockSpec(memory_space=pltpu.VMEM)
    return pl.pallas_call(
        functools.partial(gradient_kernel, parts, order),
        out_shape=(jax.ShapeDtypeStruct((chips // 2, features, width), BF),) * 2,
        in_specs=[vmem_spec] * (1 + 2 * parts),
        out_specs=(vmem_spec,) * 2,
        compiler_params=pltpu.CompilerParams(vmem_limit_bytes=VMEM_LIMIT),
        cost_estimate=pl.CostEstimate(
            flops=2 * chips * features * tokens * width, bytes_accessed=8 * 1024 * 1024, transcendentals=0
        ),
        name="gradient",
    )(grad, *own, *other)


def joint_kernel(parts, rest, *refs):
    grad, near = refs[:2]
    pieces, outs = refs[2 : 2 + 4 * parts], refs[2 + 4 * parts :]
    rows = pieces[0].shape[0]
    for out, e, i in ((outs[0], rest, 1), (outs[1], 0, 0)):
        start = 0
        for g in range(parts):
            own, other, near_own, near_other = (pieces[k * parts + g] for k in range(4))
            total = dot(grad[e, :, :rows], own[...]) + dot(grad[e, :, rows:], other[...])
            total += dot(near[i, :, :rows], near_own[...]) + dot(near[i, :, rows:], near_other[...])
            out[0, :, start : start + own.shape[1]] = total.astype(BF)
            start += own.shape[1]


def joint_gradient(grad, near, pieces, rest):
    chips, features, tokens = grad.shape
    width = sum(a.shape[1] for a in pieces[0])
    vmem_spec = pl.BlockSpec(memory_space=pltpu.VMEM)
    return pl.pallas_call(
        functools.partial(joint_kernel, len(pieces[0]), rest),
        out_shape=(jax.ShapeDtypeStruct((1, features, width), BF),) * 2,
        in_specs=[vmem_spec] * (2 + 4 * len(pieces[0])),
        out_specs=(vmem_spec,) * 2,
        compiler_params=pltpu.CompilerParams(vmem_limit_bytes=VMEM_LIMIT),
        cost_estimate=pl.CostEstimate(
            flops=2 * chips * features * tokens * width, bytes_accessed=8 * 1024 * 1024, transcendentals=0
        ),
        name="joint",
    )(grad, near, *sum(pieces, []))


def place_columns_kernel(count, *refs):
    where_ref, out = refs[0], refs[-1]
    size = refs[1].shape[2]
    for i in range(count):
        start = pl.multiple_of(where_ref[i] * size, size)
        out[:, pl.ds(start, size)] = refs[1 + i][2 * i // count]


def place_columns(slots, front, rear):
    pieces = list(front) + list(rear)
    count = len(pieces)
    _, rows, size = pieces[0].shape
    if size % HD:
        flat = jnp.stack([p[2 * i // count] for i, p in enumerate(pieces)], 0)
        flat = jnp.take(flat, jnp.argsort(slots), axis=0, mode="clip")
        return jnp.concatenate([flat[i] for i in range(count)], 1)
    vmem_spec = pl.BlockSpec(memory_space=pltpu.VMEM)
    return pl.pallas_call(
        functools.partial(place_columns_kernel, count),
        out_shape=jax.ShapeDtypeStruct((rows, count * size), BF),
        in_specs=[pl.BlockSpec(memory_space=pltpu.SMEM)] + [vmem_spec] * count,
        out_specs=vmem_spec,
        compiler_params=pltpu.CompilerParams(vmem_limit_bytes=VMEM_LIMIT),
        cost_estimate=pl.CostEstimate(flops=0, bytes_accessed=6 * 1024 * 1024, transcendentals=0),
        name="place_columns",
    )(slots.astype(jnp.int32), *pieces)


def place_rows_kernel(count, *refs):
    where_ref, pieces = refs[0], refs[1 : 1 + count]
    out, wide, sem = refs[-3:]
    size = wide.shape[1]
    copies = []
    for i in range(count):
        wide[i] = pieces[i][...].astype(F32)
        start = pl.multiple_of(where_ref[i] * size, size)
        copies.append(pltpu.make_async_copy(wide.at[i], out.at[pl.ds(start, size), :], sem.at[i]))
        copies[-1].start()
    for copy in copies:
        copy.wait()


def place_rows(slots, pieces, shape, before=None):
    count = len(pieces)
    extra = [] if before is None else [before]
    any_spec = pl.BlockSpec(memory_space=pl.ANY)
    return pl.pallas_call(
        functools.partial(place_rows_kernel, count),
        out_shape=jax.ShapeDtypeStruct(shape, F32),
        in_specs=[pl.BlockSpec(memory_space=pltpu.SMEM)]
        + [pl.BlockSpec(memory_space=pltpu.VMEM)] * count
        + [any_spec] * len(extra),
        out_specs=any_spec,
        scratch_shapes=[pltpu.VMEM((count, *pieces[0].shape), F32), pltpu.SemaphoreType.DMA((count,))],
        input_output_aliases={1 + count: 0} if extra else {},
        compiler_params=pltpu.CompilerParams(vmem_limit_bytes=VMEM_LIMIT),
        cost_estimate=pl.CostEstimate(flops=0, bytes_accessed=count * 1572864, transcendentals=0),
        name="place_rows",
    )(slots.astype(jnp.int32), *pieces, *extra)


def local(n_seq, n_head, prefix_k, prefix_v, queries, suffix_k, suffix_v, residual, out_weight,
          norm_gain, value_weight, prompt_of, suffix_len, return_table, return_index):
    chips = n_seq // 2
    bits = [1 << b for b in range(chips.bit_length() - 1)]
    rows = queries.shape[0]
    local_width = residual.shape[1]
    model = local_width * n_head
    kv_heads = prefix_k.shape[2] // HD
    group = queries.shape[1] // (kv_heads * HD)
    positions = prefix_k.shape[1]
    block_len = positions // n_seq
    seq = lax.axis_index(SEQ)
    plane = lax.axis_index(HEAD)
    chip, core = seq // 2, seq % 2

    def seq_send(x, mask):
        return lax.ppermute(x, SEQ, xor_perm(n_seq, mask))

    def partner(x):
        return seq_send(x, 1)

    def chip_send(x, bit):
        return seq_send(x, 2 * bit)

    def plane_send(x, step):
        return lax.ppermute(x, HEAD, shift_perm(n_head, step))

    def next_plane(step):
        return (plane + step) % n_head

    def plane_send(x, step):
        return lax.ppermute(x, HEAD, shift_perm(n_head, step))

    def next_plane(step):
        return (plane + step) % n_head

    weight_rows = out_weight.shape[0] // n_head
    w_own = []
    for t in range(n_head):
        piece = lax.dynamic_slice_in_dim(out_weight, next_plane(t) * weight_rows, weight_rows, 0)
        w_own.append(plane_send(piece, t) if t else piece)

    res = residual.reshape(rows, 2, n_head, weight_rows)
    mine = lax.dynamic_index_in_dim(res, core, 1, keepdims=False)
    yours = lax.dynamic_index_in_dim(res, 1 - core, 1, keepdims=False)
    theirs = partner(yours)
    res = []
    for t in range(n_head):
        piece = jnp.stack(
            [lax.dynamic_index_in_dim(x, next_plane(t), 1, keepdims=False) for x in (mine, theirs)], 0
        )
        res.append(plane_send(piece, t) if t else piece)

    gain_weight = norm_gain * value_weight
    gain = gain_weight.reshape(chips, 2, n_head, weight_rows)
    gain = lax.dynamic_index_in_dim(gain, core, 1, keepdims=False)
    gain = lax.dynamic_index_in_dim(gain, plane, 1, keepdims=False)

    bins = return_table.shape[0]
    one_hot = return_index[:, None] == jnp.arange(bins)[None, :]
    target = jnp.sum(jnp.where(one_hot, return_table[None, :], 0.0), 1)
    target_other = partner(target)

    pick = prompt_of.astype(jnp.int32)
    attn = []
    caches = ()
    for head in range(kv_heads):
        cut = slice(head * HD, (head + 1) * HD)
        both = jnp.stack([x[0, :, cut].reshape(n_seq, block_len, HD) for x in (prefix_k, prefix_v)], 1)
        if head:
            both = tie(both, kv)
        came = lax.all_to_all(both, SEQ, split_axis=0, concat_axis=0, tiled=True)
        if head:
            came = tie(came, attn[-1])
        chosen, caches = route(pick, came, head, kv_heads, caches)
        kv = lax.all_to_all(chosen, SEQ, split_axis=0, concat_axis=0, tiled=True)
        last = head == kv_heads - 1
        count = max(group // 2, 1) if last else group
        for step, first in enumerate(range(0, group, count)):
            if last and first + count == group:
                kv, *res = lax.optimization_barrier((kv, *res))
            tile = 2 * TILE if last and first + count == group else TILE
            attn.append(attention(queries, kv, suffix_k, suffix_v, head, group, first, count, tile))
    cache_k, cache_v = caches

    half = n_head // 2
    w_own = list(lax.optimization_barrier((*w_own, attn[0]))[:-1])
    w_late = list(lax.optimization_barrier((*w_own, chosen))[:-1])
    weights = [w_own] + [None] * (chips - 1)
    for e in sorted(range(1, chips), key=lambda v: bin(v).count("1")):
        low, high = e & -e, 1 << (e.bit_length() - 1)
        got = [None] * n_head
        turn = [*range(half, n_head), *range(half)] if low == 1 else [*range(n_head)]
        for t in turn:
            if low == high:
                got[t] = chip_send(w_late[t], e)
            else:
                bit = low if t < half else high
                got[t] = chip_send(weights[e ^ bit][t], bit)
        weights[e] = got

    parts = len(attn)
    own = [[None] * parts for _ in range(n_head)]
    other = [[None] * parts for _ in range(n_head)]
    for g in range(parts):
        for t in range(n_head):
            if not t:
                own[t][g] = attn[g]
            elif g + 2 < parts or parts == 3 and not g:
                own[t][g] = plane_send(own[t - 1][g], 1)
            else:
                own[t][g] = plane_send(attn[g], t)
            other[t][g] = partner(own[t][g])

    early = {1: bits[0], 2: bits[1]} if len(bits) == 2 and n_head == 4 else {}
    near_attn = {}
    for t, bit in early.items():
        mine, theirs = [], []
        for g in range(parts):
            mine.append(chip_send(own[t][g], bit))
            theirs.append(partner(mine[-1]))
        near_attn[t] = mine, theirs

    where = jnp.stack([chip, plane]).astype(jnp.int32)
    weights = sum(weights, [])
    sends = [(bit, sum(bits)) for bit in early.values()]
    *h_outs, h_flip, sums = project(where, own, other, weights, res, gain[:, :, None], sends)
    h_outs, flips = h_outs[:n_head], h_outs[n_head:]

    near_flip = {}
    for (t, bit), flip in zip(early.items(), flips):
        near_flip[t] = chip_send(flip, bit)

    back = []
    for t in range(n_head):
        back.append(plane_send(h_outs[t], t) if t else h_outs[0])
    rest = [partner(piece) for piece in back]
    slots = [side * n_head + next_plane(-t) for side in (core, 1 - core) for t in range(n_head)]
    hidden = place_columns(jnp.stack(slots), back, rest)

    yours = partner(sums[:4])
    totals = sums[:4] + jnp.concatenate([yours[2:], yours[:2]], 0)
    step = 1
    while step < n_head:
        totals = totals + lax.ppermute(totals, HEAD, xor_perm(n_head, step))
        step *= 2
    square_sum = jnp.concatenate([totals[0], totals[2]])
    weighted_sum = jnp.concatenate([totals[1], totals[3]])
    inverse = lax.rsqrt(square_sum / model + EPSILON)
    value_rows = weighted_sum * inverse
    targets = jnp.concatenate([target, target_other])
    position = jnp.arange(rows)
    live = jnp.concatenate([position < suffix_len[seq], position < suffix_len[seq ^ 1]])
    error = jnp.where(live, value_rows - targets, 0.0)
    first_term = error * inverse
    second_term = error * (weighted_sum * inverse * inverse * inverse) / model
    gain_near = jnp.take(gain, chip ^ jnp.arange(chips), axis=0, mode="clip")

    def hidden_grad(terms, gains, flip):
        return (
            terms[0][None, None, :] * gains[:, :, None] - terms[1][None, None, :] * flip.astype(F32)
        ).astype(BF)

    terms = jnp.stack([first_term, second_term], 0)
    grad = hidden_grad(terms, gain_near, h_flip)
    near_grad = {}
    for t, bit in early.items():
        near_terms = chip_send(terms, bit)
        gains = jnp.stack([gain_near[0], gain_near[sum(bits) ^ bit]], 0)
        near_grad[t] = hidden_grad(near_terms, gains, near_flip[t])

    final = []
    turns = sorted(range(n_head), key=lambda t: (t != 0, t not in early, -t))
    for t in turns:
        turn = bits if t % 2 else bits[::-1]
        order = [sum(bit for k, bit in enumerate(turn[::-1]) if i >> k & 1) for i in range(chips)]
        if t in early:
            pieces = [own[t], other[t], *near_attn[t]]
            send, keep = joint_gradient(grad, near_grad[t], pieces, turn[1])
        else:
            send, keep = gradient(grad, own[t], other[t], order)
        for stage, bit in enumerate(turn):
            if t in early and not stage:
                continue
            got = chip_send(send, bit)
            half = keep.shape[0] // 2
            if half:
                send = (keep[half:].astype(F32) + got[half:].astype(F32)).astype(BF)
                keep = (keep[:half].astype(F32) + got[:half].astype(F32)).astype(BF)
            else:
                keep = (keep.astype(F32) + got.astype(F32)).astype(BF)
        final.append(plane_send(keep[0], -t) if t else keep[0])
    late = turns.index(n_head - 1)
    early = [i for i in range(n_head) if i != late]
    shape = (n_head * weight_rows, out_weight.shape[1])
    grad_out = place_rows(jnp.stack([next_plane(turns[i]) for i in early]), [final[i] for i in early], shape)
    grad_out = place_rows(next_plane(turns[late])[None], [final[late]], shape, grad_out)
    return (cache_k, cache_v, hidden, value_rows[:rows], grad_out)


def solution(mesh):
    in_specs = (
        P(SEQ, None, HEAD),
        P(SEQ, None, HEAD),
        P(SEQ, HEAD),
        P(SEQ, HEAD),
        P(SEQ, HEAD),
        P(SEQ, HEAD),
        P(SEQ, HEAD),
        P(),
        P(),
        P(),
        P(),
        P(),
        P(SEQ),
    )
    out_specs = (
        P(None, SEQ, HEAD),
        P(None, SEQ, HEAD),
        P(SEQ, HEAD),
        P(SEQ),
        P(SEQ, HEAD),
    )
    body = functools.partial(local, mesh.shape[SEQ], mesh.shape[HEAD])

    return jax.shard_map(body, mesh=mesh, in_specs=in_specs, out_specs=out_specs, check_vma=False)
```
